128 devices in a mesh: lon: 16 (over y_hi, x, core), lat: 8 (over y_lo, z).
Axes of the slice: x: 4, y: 4 (y_hi: 2, y_lo: 2; y = y_hi * 2 + y_lo), z: 4, core: 2. Of those that a mesh axis runs over, the one named last changes fastest.
Arguments:
- grid_state: bfloat16 [1024, 256, 384], P('lon', 'lat'), may hold values from -6 to 6
- conv_weight: bfloat16 [9, 384, 384], replicated, may hold values from -0.109375 to 0.109375
- mix_weight: bfloat16 [384, 384], replicated, may hold values from -0.3125 to 0.3125
- teacher: bfloat16 [8, 128, 256, 384], P('lat', 'lon'), may hold values from -6 to 6
- tile_mask: int32 [16, 8, 8], P('lon', 'lat'), may hold values from 0 to 1, as said below
- source_owner: int32 [8, 16, 16], P('lat'), may hold values from 0 to 15, as said below
- source_block: int32 [8, 16, 16], P('lat'), may hold values from 0 to 7
- margin_weight: float32 [8, 16, 16], P('lat', 'lon'), may hold values from 0.2 to 1
Outputs:
- next_state: bfloat16 [1024, 256, 384], P('lon', 'lat')
- misfit: bfloat16 [1024, 256, 384], P('lon', 'lat')
- grad_conv: float32 [9, 384, 384], replicated
- grad_mix: float32 [384, 384], replicated
The draws below stay inside these ranges and needn't reach their ends.
Inputs may be any that keep to these rules, and one draw needn't show every extreme that they name: `tile_mask`: 1 marks an ocean tile; every device holds 1 to 4 ocean tiles, and some device holds exactly 4. `source_owner`: blocks lie in the tile's own latitude row. Among the 16 entries of one device no lon index appears more than 2 times, and on every device some lon index appears exactly 2 times.
All inputs are finite; a program needn't handle non-finite values.
Results may differ from the reference program's by a relative error of at most 0.0032.
Values may be sent and summed in bfloat16 or wider, within the bound.
A program may use at most 128 MiB of HBM per device.

```python
import math
import jax
import jax.numpy as jnp
from jax import lax

C = 384
TS = 16
K = 2
BLK_DEV = 8
LX = 64
LY = 32
LON_DEVS = 16
LAT_DEVS = 8
NLON = 1024
NLAT = 256
TC = 256
TPD = 8
REQUESTS = 16
CAP = 2
OCEAN_MAX = 4


def draw_tile_mask(key, part):
    key_count = jax.random.fold_in(key, 11)
    key_busy = jax.random.fold_in(key, 12)
    key_place = jax.random.fold_in(key, 13)
    device_count = LON_DEVS * LAT_DEVS
    counts = jax.random.randint(key_count, (device_count,), 1, OCEAN_MAX + 1)
    busiest = jax.random.randint(key_busy, (), 0, device_count)
    counts = jnp.where(jnp.arange(device_count) == busiest, OCEAN_MAX, counts)
    subkeys = jax.random.split(key_place, device_count)
    places = jax.vmap(lambda subkey: jax.random.permutation(subkey, TPD))(subkeys)
    flags = (places < counts[:, None]).astype(jnp.int32)
    return flags.reshape(LON_DEVS, LAT_DEVS, TPD)


def draw_source_owner(key, part):
    peers = LON_DEVS
    wanted = TPD * K

    def one_device(subkey):
        key_main = jax.random.fold_in(subkey, 1)
        key_rest = jax.random.fold_in(subkey, 2)
        key_order = jax.random.fold_in(subkey, 3)
        main_peer = jax.random.randint(key_main, (), 0, peers)
        spread = jax.random.permutation(key_rest, CAP * (peers - 1))
        others = (main_peer + 1 + spread[:wanted - CAP] % (peers - 1)) % peers
        owners = jnp.concatenate([jnp.zeros((CAP,), jnp.int32) + main_peer, others.astype(jnp.int32)])
        order = jax.random.permutation(key_order, wanted)
        return owners[order]
    subkeys = jax.random.split(jax.random.fold_in(key, 21), LAT_DEVS * LON_DEVS)
    owners_all = jax.vmap(one_device)(subkeys)
    return owners_all.reshape(LAT_DEVS, LON_DEVS, wanted).astype(jnp.int32)


def set_ends(values, own_key, smallest, high):
    longest = values.shape.index(max(values.shape))
    spots = []
    for shift in (0, 1):
        where = [jax.random.randint(jax.random.fold_in(own_key, axis), (), 0, length) for axis, length in enumerate(values.shape)]
        where[longest] = (where[longest] + shift) % values.shape[longest]
        spots.append(tuple(where))
    return values.at[spots[0]].set(smallest).at[spots[1]].set(high)


def shard_levels(stream_key, dims, cuts, smallest, largest):
    factor_of = 1.0
    for axis_at, blocks in cuts:
        draws = jax.random.uniform(jax.random.fold_in(jax.random.fold_in(stream_key, 6), axis_at), (blocks,), jnp.float32, smallest / len(cuts), largest / len(cuts))
        factor_of = factor_of * jnp.repeat(jnp.exp(draws), dims[axis_at] // blocks).reshape((-1,) + (1,) * (len(dims) - 1 - axis_at))
    return factor_of


def centred(stream_key, extent, scale, limit, pieces=(), kind=jnp.bfloat16):
    loudness = shard_levels(stream_key, extent, pieces, -0.22, 0.18) if pieces else 1.0
    values = jax.random.normal(stream_key, extent, jnp.float32) * scale * loudness
    return jnp.minimum(jnp.maximum(values, -limit), limit).astype(kind)


def setup_inputs(seed: int = 0) -> dict:
    streams_of = jax.random.split(jax.random.key(seed), 9)
    return {
        "grid_state": centred(streams_of[0], (NLON, NLAT, C), 1.0, 6.0, ((0, 16), (1, 8))),
        "conv_weight": centred(streams_of[1], (9, C, C), (9 * C) ** -0.5, 0.109375),
        "mix_weight": centred(streams_of[2], (C, C), C ** -0.5, 0.3125),
        "teacher": centred(streams_of[3], (LAT_DEVS, LON_DEVS * BLK_DEV, TC, C), 1.0, 6.0, ((0, 8), (1, 16))),
        "tile_mask": draw_tile_mask(jax.random.fold_in(streams_of[8], 71), 0),
        "source_owner": draw_source_owner(jax.random.fold_in(streams_of[8], 71), 0),
        "source_block": set_ends(jax.random.randint(streams_of[6], (LAT_DEVS, LON_DEVS, REQUESTS), 0, BLK_DEV), jax.random.fold_in(streams_of[6], 1), 0, BLK_DEV - 1).astype(jnp.int32),
        "margin_weight": jnp.clip(0.2 + 0.8 * jax.random.uniform(streams_of[7], (LAT_DEVS, LON_DEVS, REQUESTS), jnp.float32) ** shard_levels(streams_of[7], (LAT_DEVS, LON_DEVS, REQUESTS), ((0, 8), (1, 16)), -0.2, 0.2), 0.2, 1.0),
    }


def block_step(windows, centre, target, keep_rows, conv_weight, mix_weight, scale):
    count, height, breadth, chans = windows.shape
    height = height - 2
    breadth = breadth - 2
    row_count = count * height * breadth

    def shifted(offset):
        step_lon, step_lat = divmod(offset, 3)
        return windows[:, step_lon:step_lon + height, step_lat:step_lat + breadth, :].reshape(row_count, chans)
    pre = jnp.zeros((row_count, chans), jnp.float32)
    for offset in range(9):
        pre = pre + jnp.dot(shifted(offset), conv_weight[offset], preferred_element_type=jnp.float32)
    sigmoid_pre = jax.nn.sigmoid(pre)
    hidden = (pre * sigmoid_pre).astype(jnp.bfloat16)
    full_state = centre.astype(jnp.float32) + jnp.dot(hidden, mix_weight, preferred_element_type=jnp.float32)
    next_state = (keep_rows * full_state).astype(jnp.bfloat16)
    error = keep_rows * (full_state - target)
    misfit = error.astype(jnp.bfloat16)
    scaled = (error * scale).astype(jnp.bfloat16)
    grad_mix = lax.dot_general(hidden, scaled, (((0,), (0,)), ((), ())), preferred_element_type=jnp.float32)
    back_grad = lax.dot_general(scaled, mix_weight, (((1,), (1,)), ((), ())), preferred_element_type=jnp.float32)
    dpre = (back_grad * sigmoid_pre * (1.0 + pre * (1.0 - sigmoid_pre))).astype(jnp.bfloat16)
    grad_conv = jnp.stack([lax.dot_general(shifted(offset), dpre, (((0,), (0,)), ((), ())), preferred_element_type=jnp.float32) for offset in range(9)])
    return (next_state, misfit, grad_conv, grad_mix)

def reference(grid_state, conv_weight, mix_weight, teacher, tile_mask, source_owner, source_block, margin_weight):
    tiles_lon = LX // TS
    tiles_lat = LY // TS
    lon_wide = jnp.concatenate([grid_state[-1:], grid_state, grid_state[:1]], axis=0)
    padded = jnp.pad(lon_wide, ((0, 0), (1, 1), (0, 0)))

    def row_target(packed):
        teach_row, owners, blocks, weights = packed
        picked = teach_row[owners * BLK_DEV + blocks]
        mixed = picked.astype(jnp.float32) * weights[:, :, None, None]
        return lax.optimization_barrier(jnp.sum(mixed.reshape(LON_DEVS, TPD, K, TC, C), axis=2))
    targets = lax.map(row_target, (teacher, source_owner, source_block, margin_weight))
    targets = targets.reshape(LAT_DEVS, LON_DEVS, tiles_lon, tiles_lat, TS, TS, C)
    targets = jnp.transpose(targets, (1, 2, 4, 0, 3, 5, 6)).reshape(NLON * NLAT, C)
    ocean = tile_mask.astype(jnp.float32).reshape(LON_DEVS, LAT_DEVS, tiles_lon, tiles_lat)
    ocean = jnp.broadcast_to(ocean[:, :, :, :, None, None], (LON_DEVS, LAT_DEVS, tiles_lon, tiles_lat, TS, TS))
    ocean = jnp.transpose(ocean, (0, 2, 4, 1, 3, 5)).reshape(NLON * NLAT, 1)
    scale = 1.0 / math.sqrt(NLON * NLAT)
    next_state, misfit, grad_conv, grad_mix = block_step(padded[None], grid_state.reshape(NLON * NLAT, C), targets, ocean, conv_weight, mix_weight, scale)
    return (next_state.reshape(NLON, NLAT, C), misfit.reshape(NLON, NLAT, C), grad_conv, grad_mix)
```

```python
import functools
import math

import jax
import jax.numpy as jnp
from jax import lax
from jax.experimental import pallas as pl
from jax.experimental.pallas import tpu as pltpu
from jax.sharding import PartitionSpec as P

TS = 16
K = 2
SLOTS = 4
C = 384
NX = 4
NCH = 4
CR = 128 // NCH
HALF = 2048
MESH = pl.DeviceIdType.MESH
F32 = jnp.float32
BF16 = jnp.bfloat16


def my_place():
    lon = lax.axis_index("lon")
    lat = lax.axis_index("lat")
    core = lax.rem(lon, 2)
    x = lax.rem(lax.div(lon, 2), 4)
    y = lax.div(lon, 8) * 2 + lax.div(lat, 4)
    z = lax.rem(lat, 4)
    return x, y, z, core


def device(x, y, z, core):
    x = lax.rem(x + 8, 4)
    y = lax.rem(y + 8, 4)
    z = lax.rem(z + 8, 4)
    return (lax.div(y, 2) * 8 + x * 2 + core, lax.rem(y, 2) * 4 + z)


def remote(src, dst, send, recv, where):
    return pltpu.make_async_remote_copy(
        src_ref=src, dst_ref=dst, send_sem=send, recv_sem=recv, device_id=where, device_id_type=MESH
    )


def greet(devices):
    barrier = pltpu.get_barrier_semaphore()
    for where in devices:
        pl.semaphore_signal(barrier, inc=1, device_id=where, device_id_type=MESH)
    pl.semaphore_wait(barrier, len(devices))


def exchange_kernel(
    meta_i, meta_w, edges, grid, teacher,
    sums, halo_lon, halo_lat, corner,
    mi_buf, mw_buf, mi_smem, mw_smem, relay_y, send, relay_x,
    sem_m, sem_ms, sem_h, sem_own, sem_core, sem_h1, sem_h2, sem_x1, sem_x2, sem_x3, sem_x0, *raw,
):
    x, y, z, core = my_place()
    other = 1 - core
    lon = lax.axis_index("lon")
    lat = lax.axis_index("lat")
    lon_up, lon_dn = lax.rem(lon + 1, 16), lax.rem(lon + 15, 16)
    lat_up, lat_dn = lax.rem(lat + 1, 8), lax.rem(lat + 7, 8)

    def sgn(way):
        return 1 if way == 0 else -1

    greet(
        [device(x, y, z, other)]
        + [device(x, y + s, z, h) for s in (1, -1) for h in (0, 1)]
        + [device(x + s, y, z, h) for s in (1, 2, 3) for h in (0, 1)]
        + [(lon_up, lat), (lon_dn, lat), (lon, lat_up), (lon, lat_dn)]
        + [(lon_up, lat_up), (lon_up, lat_dn), (lon_dn, lat_up), (lon_dn, lat_dn)]
    )

    def rows(half, ch):
        return pl.ds(pl.multiple_of(half * 128 + ch * CR, CR), CR)

    hop1, hop2, own, cross, fwd_x, all_x = {}, {}, {}, {}, {}, []

    def start_hop1(ch):
        for way in (0, 1):
            for h in (0, 1):
                copy = remote(
                    teacher.at[0, way * 4 : way * 4 + 4, rows(h, ch), :],
                    relay_y.at[ch, way, pl.ds(core * 4, 4)],
                    sem_h1.at[0, ch, way, h],
                    sem_h1.at[1, ch, way, core],
                    device(x, y + sgn(way), z, h),
                )
                copy.start()
                hop1[ch, way, h] = copy

    def arrived_hop1(ch, way, src_core):
        return remote(
            teacher.at[0, way * 4 : way * 4 + 4, rows(0, ch), :],
            relay_y.at[ch, way, src_core * 4 : src_core * 4 + 4],
            sem_h1.at[0, ch, way, src_core],
            sem_h1.at[1, ch, way, src_core],
            device(x, y - sgn(way), z, src_core),
        )

    def start_hop2(ch):
        for way in (0, 1):
            for src_core in (0, 1):
                arrived_hop1(ch, way, src_core).wait_recv()
            copy = remote(
                relay_y.at[ch, way],
                raw[ch].at[16 + way * 8 : 24 + way * 8],
                sem_h2.at[0, ch, way],
                sem_h2.at[1, ch, way],
                device(x, y + sgn(way), z, core),
            )
            copy.start()
            hop2[ch, way] = copy

    start_hop1(0)

    metas = []
    for d in (1, 2, 3, 0):
        for c in (0, 1):
            if d == 0 and c == 1:
                continue
            where = device(x + d, y, z, c if d else other)
            for kind, (src, dst) in enumerate(((meta_i, mi_buf), (meta_w, mw_buf))):
                tag = core if d else 0
                copy = remote(
                    src,
                    dst.at[(4 - d) % 4, core],
                    sem_m.at[0, kind, d, c],
                    sem_m.at[1, kind, (4 - d) % 4, tag],
                    where,
                )
                copy.start()
                metas.append(copy)
    mi_buf[0, core] = meta_i[...]
    mw_buf[0, core] = meta_w[...]

    for ch in range(NCH):
        copy = pltpu.make_async_copy(
            teacher.at[0, :, rows(core, ch), :], raw[ch].at[pl.ds(core * 8, 8)], sem_own.at[ch]
        )
        copy.start()
        own[ch] = copy
        copy = remote(
            teacher.at[0, :, rows(other, ch), :],
            raw[ch].at[pl.ds(core * 8, 8)],
            sem_core.at[0, ch],
            sem_core.at[1, ch],
            device(x, y, z, other),
        )
        copy.start()
        cross[ch] = copy

    if NCH > 1:
        start_hop1(1)

    halos = []
    for n, (src, dst, where) in enumerate(
        (
            (grid.at[63], halo_lon.at[0], (lon_up, lat)),
            (grid.at[0], halo_lon.at[1], (lon_dn, lat)),
            (edges.at[1], halo_lat.at[0], (lon, lat_up)),
            (edges.at[0], halo_lat.at[1], (lon, lat_dn)),
            (edges.at[1, 48:64], corner.at[0], (lon_up, lat_up)),
            (edges.at[0, 48:64], corner.at[1], (lon_up, lat_dn)),
            (edges.at[1, 0:16], corner.at[2], (lon_dn, lat_up)),
            (edges.at[0, 0:16], corner.at[3], (lon_dn, lat_dn)),
        )
    ):
        copy = remote(src, dst, sem_h.at[0, n], sem_h.at[1, n], where)
        copy.start()
        halos.append(copy)

    for s in range(4):
        for c in (0, 1):
            if s == 0 and c == 1:
                continue
            for kind, (src, dst) in enumerate(((meta_i, mi_buf), (meta_w, mw_buf))):
                remote(
                    src, dst.at[s, c if s else other],
                    sem_m.at[0, kind, s, c], sem_m.at[1, kind, s, c], device(x + s, y, z, c),
                ).wait_recv()
    to_smem = [
        pltpu.make_async_copy(mi_buf, mi_smem, sem_ms.at[0]),
        pltpu.make_async_copy(mw_buf, mw_smem, sem_ms.at[1]),
    ]
    for copy in to_smem:
        copy.start()
    for copy in to_smem:
        copy.wait()

    def pick(d, c, t, k):
        g = mi_smem[d, c, 0, t * 2 + k]
        w = mw_smem[d, c, 0, t * 2 + k]
        owner, block = g // 8, g % 8
        o_core, o_x, o_yhi = owner % 2, (owner // 2) % 4, owner // 8
        near = o_core * 8 + block
        far = 16 + (block // 4) * 8 + o_core * 4 + block % 4
        where = jnp.where(o_yhi == y // 2, near, far)
        return where, jnp.where(o_x == x, w, 0.0)

    def compute(ch):
        own[ch].wait()
        cross[ch].wait_recv()
        for way in (0, 1):
            hop2[ch, way].wait_recv()
        for d in range(4):

            def one(n, carry, d=d):
                if d == 2:
                    c, t = (n // 2) % 2, (n // 4) * 2 + n % 2
                else:
                    c, t = n // 4, n % 4
                i0, w0 = pick(d, c, t, 0)
                i1, w1 = pick(d, c, t, 1)
                total = w0 * raw[ch][i0].astype(F32) + w1 * raw[ch][i1].astype(F32)
                send[ch, d * 8 + n] = total.astype(BF16)
                return carry

            lax.fori_loop(0, 8, one, 0)

    def go(copy):
        copy.start()
        all_x.append(copy)

    def start_x(ch):
        for way, d in ((0, 2), (1, 2)):
            copy = remote(
                send.at[ch, 16 + way * 4 : 20 + way * 4],
                relay_x.at[ch, way],
                sem_x2.at[0, ch, way],
                sem_x2.at[1, ch, way],
                device(x + sgn(way), y, z, core),
            )
            copy.start()
            fwd_x[ch, way] = copy
        for d in (1, 3):
            for c in (0, 1):
                go(
                    remote(
                        send.at[ch, d * 8 + c * 4 : d * 8 + c * 4 + 4],
                        sums.at[4 - d, :, rows(core, ch), :],
                        sem_x1.at[0, ch, d // 2, c],
                        sem_x1.at[1, ch, d // 2, core],
                        device(x + d, y, z, c),
                    )
                )
        go(
            remote(
                send.at[ch, pl.ds(other * 4, 4)],
                sums.at[0, :, rows(core, ch), :],
                sem_x0.at[0, ch],
                sem_x0.at[1, ch],
                device(x, y, z, other),
            )
        )
        copy = pltpu.make_async_copy(
            send.at[ch, pl.ds(core * 4, 4)], sums.at[0, :, rows(core, ch), :], sem_x0.at[2, ch]
        )
        copy.start()
        own[ch, "x"] = copy

    def forward_x(ch):
        for way in (0, 1):
            fwd_x[ch, way].wait_recv()
            for c in (0, 1):
                go(
                    remote(
                        relay_x.at[ch, way, c * 2 : c * 2 + 2],
                        sums.at[2, way * 2 : way * 2 + 2, rows(core, ch), :],
                        sem_x3.at[0, ch, way, c],
                        sem_x3.at[1, ch, way, core],
                        device(x + sgn(way), y, z, c),
                    )
                )

    for ch in range(NCH):
        start_hop2(ch)
        if ch + 2 < NCH:
            start_hop1(ch + 2)
        if ch >= 1:
            compute(ch - 1)
            start_x(ch - 1)
        if ch >= 2:
            forward_x(ch - 2)
    compute(NCH - 1)
    start_x(NCH - 1)
    if NCH > 1:
        forward_x(NCH - 2)
    forward_x(NCH - 1)

    for copy in all_x:
        copy.wait_send()
    for ch in range(NCH):
        for d in (1, 3):
            for h in (0, 1):
                remote(
                    send.at[ch, 0:4],
                    sums.at[4 - d, :, rows(h, ch), :],
                    sem_x1.at[0, ch, d // 2, h],
                    sem_x1.at[1, ch, d // 2, h],
                    device(x + 1, y, z, h),
                ).wait_recv()
        remote(
            send.at[ch, 0:4],
            sums.at[0, :, rows(other, ch), :],
            sem_x0.at[0, ch],
            sem_x0.at[1, ch],
            device(x, y, z, other),
        ).wait_recv()
        own[ch, "x"].wait()
        for way in (0, 1):
            fwd_x[ch, way].wait_send()
            hop2[ch, way].wait_send()
            for h in (0, 1):
                hop1[ch, way, h].wait_send()
                remote(
                    relay_x.at[ch, way, 0:2],
                    sums.at[2, way * 2 : way * 2 + 2, rows(h, ch), :],
                    sem_x3.at[0, ch, way, h],
                    sem_x3.at[1, ch, way, h],
                    device(x + 1, y, z, h),
                ).wait_recv()
        cross[ch].wait_send()
    for copy in metas:
        copy.wait_send()
    for copy in halos:
        copy.wait()


def exchange(meta_i, meta_w, edges, grid, teacher):
    anywhere = pl.BlockSpec(memory_space=pl.ANY)
    vmem = pl.BlockSpec(memory_space=pltpu.VMEM)
    dma = pltpu.SemaphoreType.DMA
    return pl.pallas_call(
        exchange_kernel,
        out_shape=(
            jax.ShapeDtypeStruct((4, SLOTS, 256, C), BF16),
            jax.ShapeDtypeStruct((2, 32, C), BF16),
            jax.ShapeDtypeStruct((2, 64, C), BF16),
            jax.ShapeDtypeStruct((4, 16, C), BF16),
        ),
        in_specs=[vmem, vmem, anywhere, anywhere, anywhere],
        out_specs=(anywhere,) * 4,
        scratch_shapes=[
            pltpu.VMEM((4, 2, 8, 128), jnp.int32),
            pltpu.VMEM((4, 2, 8, 128), F32),
            pltpu.SMEM((4, 2, 8, 128), jnp.int32),
            pltpu.SMEM((4, 2, 8, 128), F32),
            pltpu.VMEM((NCH, 2, 8, CR, C), BF16),
            pltpu.VMEM((NCH, 32, CR, C), BF16),
            pltpu.VMEM((NCH, 2, 4, CR, C), BF16),
            dma((2, 2, 4, 2)),
            dma((2,)),
            dma((2, 8)),
            dma((NCH,)),
            dma((2, NCH)),
            dma((2, NCH, 2, 2)),
            dma((2, NCH, 2)),
            dma((2, NCH, 2, 2)),
            dma((2, NCH, 2)),
            dma((2, NCH, 2, 2)),
            dma((3, NCH)),
        ]
        + [pltpu.VMEM((32, CR, C), BF16)] * NCH,
        compiler_params=pltpu.CompilerParams(collective_id=0, has_side_effects=True),
    )(meta_i, meta_w, edges, grid, teacher)


def block_kernel(
    info, grid, halo_lon, halo_lat, corner, sums, conv, mix,
    next_ref, misfit_ref, own_ref, oth_ref,
    pad, lat_buf, cor_buf, xs, dp, hid, sc, grads, sem,
    *, scale,
):
    i = pl.program_id(0)
    core = info[16]
    low_ok, high_ok = info[17], info[18]

    @pl.when(i == 0)
    def _():
        copies = [
            pltpu.make_async_copy(grid, pad.at[1:65, 16:48], sem.at[0]),
            pltpu.make_async_copy(halo_lon.at[0], pad.at[0, 16:48], sem.at[1]),
            pltpu.make_async_copy(halo_lon.at[1], pad.at[65, 16:48], sem.at[2]),
            pltpu.make_async_copy(halo_lat, lat_buf, sem.at[3]),
            pltpu.make_async_copy(corner, cor_buf, sem.at[4]),
        ]
        for copy in copies:
            copy.start()
        xs[...] = jnp.zeros_like(xs)
        dp[...] = jnp.zeros_like(dp)
        hid[...] = jnp.zeros_like(hid)
        sc[...] = jnp.zeros_like(sc)
        for copy in copies:
            copy.wait()
        low = low_ok.astype(F32)
        high = high_ok.astype(F32)
        low_rows = (lat_buf[0].astype(F32) * low).reshape(64, 1, C)
        high_rows = (lat_buf[1].astype(F32) * high).reshape(64, 1, C)
        pad[1:65, 0:16] = jnp.broadcast_to(low_rows, (64, 16, C)).astype(BF16)
        pad[1:65, 48:64] = jnp.broadcast_to(high_rows, (64, 16, C)).astype(BF16)
        for n, (row, at, side, ok) in enumerate(
            ((15, 0, 0, low), (15, 0, 48, high), (0, 65, 0, low), (0, 65, 48, high))
        ):
            value = cor_buf[n].astype(F32)[row : row + 1] * ok
            pad[at, side : side + 16] = jnp.broadcast_to(value, (16, C)).astype(BF16)

    a, b = i // 2, i % 2
    ocean = info[i] == 1
    slot = info[8 + i]

    @pl.when(jnp.logical_not(ocean))
    def _():
        next_ref[...] = jnp.zeros_like(next_ref)
        misfit_ref[...] = jnp.zeros_like(misfit_ref)

    @pl.when(ocean)
    def _():
        def shift(line, carry):
            row = pad[a * 16 + line, pl.ds(pl.multiple_of(b * 16, 16), 48), :].astype(F32)
            at = pl.ds(pl.multiple_of(line * 16, 16), 16)
            xs[0, slot, at, :] = pltpu.roll(row, 1, 0)[16:32].astype(BF16)
            xs[1, slot, at, :] = row[16:32].astype(BF16)
            xs[2, slot, at, :] = pltpu.roll(row, 47, 0)[16:32].astype(BF16)
            return carry

        lax.fori_loop(0, 18, shift, 0)
        pre = jnp.zeros((256, C), F32)
        for tap in range(9):
            lon_step, lat_step = divmod(tap, 3)
            pre = pre + jnp.dot(
                xs[lat_step, slot, lon_step * 16 : lon_step * 16 + 256, :],
                conv[tap],
                preferred_element_type=F32,
            )
        sig = jax.nn.sigmoid(pre)
        hidden = (pre * sig).astype(BF16)
        full = xs[1, slot, 16:272, :].astype(F32) + jnp.dot(
            hidden, mix[...], preferred_element_type=F32
        )
        target = sums[0, slot].astype(F32)
        for n in range(1, 4):
            target = target + sums[n, slot].astype(F32)
        error = full - target
        next_ref[...] = full.astype(BF16).reshape(16, 16, C)
        misfit_ref[...] = error.astype(BF16).reshape(16, 16, C)
        scaled = (error * scale).astype(BF16)
        back = lax.dot_general(
            scaled, mix[...], (((1,), (1,)), ((), ())), preferred_element_type=F32
        )
        hid[slot] = hidden
        sc[slot] = scaled
        dp[slot] = (back * sig * (1.0 + pre * (1.0 - sig))).astype(BF16)

    @pl.when(i == pl.num_programs(0) - 1)
    def _():
        contract = (((0,), (0,)), ((), ()))
        dpre = dp[...].reshape(1024, C)
        for tap in range(9):
            lon_step, lat_step = divmod(tap, 3)
            grads[tap * C : (tap + 1) * C, :] = lax.dot_general(
                xs[lat_step, :, lon_step * 16 : lon_step * 16 + 256, :].reshape(1024, C),
                dpre,
                contract,
                preferred_element_type=F32,
            )
        grads[9 * C : 10 * C, :] = lax.dot_general(
            hid[...].reshape(1024, C), sc[...].reshape(1024, C), contract, preferred_element_type=F32
        )
        grads[10 * C : 2 * HALF, :] = jnp.zeros((2 * HALF - 10 * C, C), F32)

        def move(n, carry):
            at = pl.ds(pl.multiple_of(n * 64, 64), 64)
            own_ref[at, :] = grads[pl.ds(pl.multiple_of(core * HALF + n * 64, 64), 64), :]
            oth_ref[at, :] = grads[
                pl.ds(pl.multiple_of((1 - core) * HALF + n * 64, 64), 64), :
            ].astype(BF16)
            return carry

        lax.fori_loop(0, HALF // 64, move, 0)


def block(info, grid, halo_lon, halo_lat, corner, sums, conv, mix, scale):
    anywhere = pl.BlockSpec(memory_space=pl.ANY)
    vmem = pl.BlockSpec(memory_space=pltpu.VMEM)
    tile = pl.BlockSpec((TS, TS, C), lambda i, info: (i // 2, i % 2, 0))
    dma = pltpu.SemaphoreType.DMA
    return pl.pallas_call(
        functools.partial(block_kernel, scale=scale),
        out_shape=(
            jax.ShapeDtypeStruct((64, 32, C), BF16),
            jax.ShapeDtypeStruct((64, 32, C), BF16),
            jax.ShapeDtypeStruct((HALF, C), F32),
            jax.ShapeDtypeStruct((HALF, C), BF16),
        ),
        grid_spec=pltpu.PrefetchScalarGridSpec(
            num_scalar_prefetch=1,
            grid=(8,),
            in_specs=[anywhere] * 4 + [vmem] * 3,
            out_specs=(tile, tile, vmem, vmem),
            scratch_shapes=[
                pltpu.VMEM((66, 64, C), BF16),
                pltpu.VMEM((2, 64, C), BF16),
                pltpu.VMEM((4, 16, C), BF16),
                pltpu.VMEM((3, SLOTS, 288, C), BF16),
                pltpu.VMEM((SLOTS, 256, C), BF16),
                pltpu.VMEM((SLOTS, 256, C), BF16),
                pltpu.VMEM((SLOTS, 256, C), BF16),
                pltpu.VMEM((2 * HALF, C), F32),
                dma((5,)),
            ],
        ),
        compiler_params=pltpu.CompilerParams(
            dimension_semantics=("arbitrary",), vmem_limit_bytes=60 * 1024 * 1024
        ),
    )(info, grid, halo_lon, halo_lat, corner, sums, conv, mix)


def reduce_kernel(
    own, oth, out,
    rc, s1, r1, a1, r2, a2, r3, obuf,
    sem_c, sem_1, sem_2, sem_3, sem_g3, sem_g2, sem_g1, sem_gc, sem_o,
):
    x, y, z, core = my_place()
    place = (x, y, z)
    other = 1 - core

    def peer(dim, r):
        at = list(place)
        at[dim] = at[dim] + r
        return device(at[0], at[1], at[2], core)

    partner = device(x, y, z, other)
    greet([partner] + [peer(d, r) for d in range(3) for r in (1, 2, 3)])

    def col(q):
        return pl.ds(q * 128, 128)

    def at1(q, r):
        return pl.ds(pl.multiple_of(lax.rem(place[q] + r, 4) * 512, 512), 512)

    pend = []

    def go(copy):
        copy.start()
        pend.append(copy)
        return copy

    first = {}
    for r in (2, 1, 3, 0):
        for q in range(3):
            first[r, q] = go(
                remote(
                    oth.at[at1(q, r), col(q)], rc.at[at1(q, r), col(q)],
                    sem_c.at[0, r, q], sem_c.at[1, r, q], partner,
                )
            )
    one = {}
    for r in (2, 1, 3):
        for q in range(3):
            first[r, q].wait_recv()
            s1[r - 1, q] = (own[at1(q, r), col(q)] + rc[at1(q, r), col(q)].astype(F32)).astype(BF16)
            one[r, q] = go(
                remote(
                    s1.at[r - 1, q], r1.at[r - 1, q], sem_1.at[0, r - 1, q], sem_1.at[1, r - 1, q],
                    peer(q, r),
                )
            )
    for q in range(3):
        first[0, q].wait_recv()
        a1[q] = own[at1(q, 0), col(q)] + rc[at1(q, 0), col(q)].astype(F32)
    two = {}
    for q in range(3):
        for r in (1, 2, 3):
            one[r, q].wait_recv()
        a1[q] = a1[q] + (
            (r1[0, q].astype(F32) + r1[1, q].astype(F32)) + r1[2, q].astype(F32)
        )
        d1 = (q + 1) % 3
        for r in (2, 1, 3):
            v = lax.rem(place[d1] + r, 4)
            two[r, q] = go(
                remote(
                    a1.at[q, pl.ds(pl.multiple_of(v * 128, 128), 128)], r2.at[r - 1, q],
                    sem_2.at[0, r - 1, q], sem_2.at[1, r - 1, q], peer(d1, r),
                )
            )
    three = {}
    for q in range(3):
        d1, d2 = (q + 1) % 3, (q + 2) % 3
        for r in (1, 2, 3):
            two[r, q].wait_recv()
        mine = a1[q, pl.ds(pl.multiple_of(place[d1] * 128, 128), 128), :]
        a2[q] = mine + ((r2[0, q] + r2[1, q]) + r2[2, q])
        for r in (2, 1, 3):
            v = lax.rem(place[d2] + r, 4)
            three[r, q] = go(
                remote(
                    a2.at[q, pl.ds(pl.multiple_of(v * 32, 32), 32)], r3.at[r - 1, q],
                    sem_3.at[0, r - 1, q], sem_3.at[1, r - 1, q], peer(d2, r),
                )
            )
    base = core * HALF

    def span(q, level, shift=0):
        dims = (q, (q + 1) % 3, (q + 2) % 3)
        sizes = (512, 128, 32)
        start = base
        for n in range(level):
            v = place[dims[n]]
            if n == level - 1 and shift:
                v = lax.rem(v + shift, 4)
            start = start + v * sizes[n]
        size = sizes[level - 1]
        return obuf.at[pl.ds(pl.multiple_of(start, size), size), col(q)]

    def spread(q, level, sem):
        dim = (q + level - 1) % 3
        return {
            r: go(
                remote(
                    span(q, level), span(q, level), sem.at[0, r - 1, q], sem.at[1, r - 1, q], peer(dim, r)
                )
            )
            for r in (2, 1, 3)
        }

    g3, g2, g1, gc = {}, {}, {}, {}
    for q in range(3):
        d2 = (q + 2) % 3
        for r in (1, 2, 3):
            three[r, q].wait_recv()
        mine = a2[q, pl.ds(pl.multiple_of(place[d2] * 32, 32), 32), :]
        final = mine + ((r3[0, q] + r3[1, q]) + r3[2, q])
        start = base + place[q] * 512 + place[(q + 1) % 3] * 128 + place[d2] * 32
        obuf[pl.ds(pl.multiple_of(start, 32), 32), col(q)] = final.astype(BF16)
        g3[q] = spread(q, 3, sem_g3)
    for q in range(3):
        for r in (1, 2, 3):
            g3[q][r].wait_recv()
        g2[q] = spread(q, 2, sem_g2)

    def give(q, r):
        piece = span(q, 1, r)
        gc[q, r] = go(remote(piece, piece, sem_gc.at[0, r, q], sem_gc.at[1, r, q], partner))

    for q in range(3):
        for r in (1, 2, 3):
            g2[q][r].wait_recv()
        g1[q] = spread(q, 1, sem_g1)
        give(q, 0)
    for r in (1, 3, 2):
        for q in range(3):
            g1[q][r].wait_recv()
            give(q, 4 - r)
    for r in range(4):
        for q in range(3):
            gc[q, r].wait_recv()
    copy = pltpu.make_async_copy(obuf, out, sem_o.at[0])
    copy.start()
    for item in pend:
        item.wait_send()
    copy.wait()


def reduce(own, oth):
    anywhere = pl.BlockSpec(memory_space=pl.ANY)
    vmem = pl.BlockSpec(memory_space=pltpu.VMEM)
    dma = pltpu.SemaphoreType.DMA
    return pl.pallas_call(
        reduce_kernel,
        out_shape=jax.ShapeDtypeStruct((2 * HALF, C), BF16),
        in_specs=[vmem, anywhere],
        out_specs=anywhere,
        scratch_shapes=[
            pltpu.VMEM((HALF, C), BF16),
            pltpu.VMEM((3, 3, 512, 128), BF16),
            pltpu.VMEM((3, 3, 512, 128), BF16),
            pltpu.VMEM((3, 512, 128), F32),
            pltpu.VMEM((3, 3, 128, 128), F32),
            pltpu.VMEM((3, 128, 128), F32),
            pltpu.VMEM((3, 3, 32, 128), F32),
            pltpu.VMEM((2 * HALF, C), BF16),
            dma((2, 4, 3)),
            dma((2, 3, 3)),
            dma((2, 3, 3)),
            dma((2, 3, 3)),
            dma((2, 3, 3)),
            dma((2, 3, 3)),
            dma((2, 3, 3)),
            dma((2, 4, 3)),
            dma((1,)),
        ],
        compiler_params=pltpu.CompilerParams(collective_id=1, has_side_effects=True),
    )(own, oth)


def body(
    grid_state, conv_weight, mix_weight, teacher, tile_mask, source_owner, source_block, margin_weight
):
    lon = lax.axis_index("lon")
    lat = lax.axis_index("lat")
    lon_count = lax.axis_size("lon")
    lat_count = lax.axis_size("lat")
    width_lon, width_lat, chans = grid_state.shape
    scale = 1.0 / math.sqrt(width_lon * lon_count * width_lat * lat_count)
    ocean = tile_mask[0, 0]
    upto = jnp.arange(8)[:, None] <= jnp.arange(8)[None, :]
    rank = jnp.sum(jnp.where(upto, ocean[:, None], 0), axis=0) - 1
    chosen = (ocean[None, :] == 1) & (rank[None, :] == jnp.arange(SLOTS)[:, None])
    owner = lax.dynamic_index_in_dim(source_owner[0], lon, 0, keepdims=False)
    held = lax.dynamic_index_in_dim(source_block[0], lon, 0, keepdims=False)
    wanted = (owner * teacher.shape[1] + held).reshape(8, K)
    weight = margin_weight[0, 0].reshape(8, K)
    meta_i = jnp.sum(jnp.where(chosen[:, :, None], wanted[None], 0), axis=1).reshape(1, SLOTS * K)
    meta_w = jnp.sum(jnp.where(chosen[:, :, None], weight[None], 0.0), axis=1).reshape(1, SLOTS * K)
    meta_i = jnp.pad(meta_i, ((0, 7), (0, 128 - SLOTS * K)))
    meta_w = jnp.pad(meta_w, ((0, 7), (0, 128 - SLOTS * K)))
    edges = jnp.stack([grid_state[:, 0, :], grid_state[:, -1, :]])
    sums, halo_lon, halo_lat, corner = exchange(meta_i, meta_w, edges, grid_state, teacher)
    info = jnp.concatenate(
        [
            ocean,
            jnp.clip(rank, 0, SLOTS - 1),
            jnp.stack([lon % 2, (lat > 0).astype(jnp.int32), (lat < lat_count - 1).astype(jnp.int32)]),
        ]
    ).astype(jnp.int32)
    next_state, misfit, own, oth = block(
        info, grid_state, halo_lon, halo_lat, corner, sums, conv_weight, mix_weight, scale
    )
    total = reduce(own, oth)
    grad_conv = total[: 9 * chans].astype(F32).reshape(9, chans, chans)
    grad_mix = total[9 * chans : 10 * chans].astype(F32)
    return next_state, misfit, grad_conv, grad_mix


def solution(mesh):
    in_specs = (
        P("lon", "lat", None),
        P(),
        P(),
        P("lat", "lon", None, None),
        P("lon", "lat", None),
        P("lat", None, None),
        P("lat", None, None),
        P("lat", "lon", None),
    )
    out_specs = (P("lon", "lat", None), P("lon", "lat", None), P(), P())
    return jax.shard_map(body, mesh=mesh, in_specs=in_specs, out_specs=out_specs, check_vma=False)
```

```python
import functools
import math

import jax
import jax.numpy as jnp
from jax import lax
from jax.experimental import pallas as pl
from jax.experimental.pallas import tpu as pltpu
from jax.sharding import PartitionSpec as P

TS = 16
K = 2
SLOTS = 4
C = 384
NCH = 8
CR = 128 // NCH
HALF = 2048
MESH = pl.DeviceIdType.MESH
F32 = jnp.float32
BF16 = jnp.bfloat16


def my_place():
    lon = lax.axis_index("lon")
    lat = lax.axis_index("lat")
    core = lax.rem(lon, 2)
    x = lax.rem(lax.div(lon, 2), 4)
    y = lax.div(lon, 8) * 2 + lax.div(lat, 4)
    z = lax.rem(lat, 4)
    return x, y, z, core


def device(x, y, z, core):
    x = lax.rem(x + 8, 4)
    y = lax.rem(y + 8, 4)
    z = lax.rem(z + 8, 4)
    return (lax.div(y, 2) * 8 + x * 2 + core, lax.rem(y, 2) * 4 + z)


def remote(src, dst, send, recv, where):
    return pltpu.make_async_remote_copy(
        src_ref=src, dst_ref=dst, send_sem=send, recv_sem=recv, device_id=where, device_id_type=MESH
    )


def greet(devices):
    barrier = pltpu.get_barrier_semaphore()
    for where in devices:
        pl.semaphore_signal(barrier, inc=1, device_id=where, device_id_type=MESH)
    pl.semaphore_wait(barrier, len(devices))


def step_kernel(
    mask_ref, owner_ref, block_ref, margin_ref, grid, teacher, conv, mix,
    next_out, mis_out, conv_out, mix_out,
    mi_own, mw_own, mi_buf, mw_buf, mi_smem, mw_smem, send, sums,
    pad, lat_buf, cor_buf, edge, wbuf, mbuf, xs, pre_buf, full_buf, hid, sc, dp, next_buf, mis_buf,
    grads, gb, rc, s1, r1, a1, r2, a2, r3, obuf,
    sem_in, sem_m, sem_ms, sem_h, sem_own, sem_core, sem_far, sem_x1, sem_x0,
    sem_c, sem_1, sem_2, sem_3, sem_g3, sem_g2, sem_g1, sem_gc, sem_o, *raw,
    scale,
):
    x, y, z, core = my_place()
    place = (x, y, z)
    other = 1 - core
    lon = lax.axis_index("lon")
    lat = lax.axis_index("lat")
    lon_up, lon_dn = lax.rem(lon + 1, 16), lax.rem(lon + 15, 16)
    lat_up, lat_dn = lax.rem(lat + 1, 8), lax.rem(lat + 7, 8)
    partner = device(x, y, z, other)

    def peer(dim, r):
        at = list(place)
        at[dim] = at[dim] + r
        return device(at[0], at[1], at[2], core)

    loads = [
        pltpu.make_async_copy(grid, pad.at[1:65, 16:48], sem_in.at[0]),
        pltpu.make_async_copy(conv, wbuf, sem_in.at[1]),
        pltpu.make_async_copy(mix, mbuf, sem_in.at[2]),
    ]
    for copy in loads:
        copy.start()

    greet(
        [partner, device(x, y + 2, z, other)]
        + [peer(d, r) for d in range(3) for r in (1, 2, 3)]
        + [device(x + s, y, z, other) for s in (1, 2, 3)]
        + [(lon_up, lat), (lon_dn, lat), (lon, lat_up), (lon, lat_dn)]
        + [(lon_up, lat_up), (lon_up, lat_dn), (lon_dn, lat_up), (lon_dn, lat_dn)]
    )

    def rows(half, ch):
        return pl.ds(pl.multiple_of(half * 128 + ch * CR, CR), CR)

    far, own, cross, pend = {}, {}, {}, []

    def go(copy):
        copy.start()
        pend.append(copy)
        return copy

    def start_far(ch):
        for h in (0, 1):
            far[ch, h] = go(
                remote(
                    teacher.at[0, :, rows(h, ch), :],
                    raw[ch].at[pl.ds(16 + core * 8, 8)],
                    sem_far.at[0, ch, h],
                    sem_far.at[1, ch, core],
                    device(x, y + 2, z, h),
                )
            )

    def far_arrived(ch):
        for h in (0, 1):
            remote(
                teacher.at[0, :, rows(h, ch), :],
                raw[ch].at[16 + h * 8 : 24 + h * 8],
                sem_far.at[0, ch, h],
                sem_far.at[1, ch, h],
                device(x, y + 2, z, h),
            ).wait_recv()

    start_far(0)
    start_far(1)

    count = jnp.int32(0)
    chosen = []
    for i in range(8):
        on = mask_ref[0, 0, i]
        chosen.append([(on == 1) & (count == t) for t in range(SLOTS)])
        count = count + on
    lane = lax.broadcasted_iota(jnp.int32, (8, 128), 1)
    meta_i = jnp.zeros((8, 128), jnp.int32)
    meta_w = jnp.zeros((8, 128), F32)
    for k in range(K):
        wanted = [owner_ref[0, lon, i * K + k] * 8 + block_ref[0, lon, i * K + k] for i in range(8)]
        weight = [margin_ref[0, 0, i * K + k] for i in range(8)]
        for t in range(SLOTS):
            index, value = jnp.int32(0), jnp.float32(0)
            for i in range(8):
                index = jnp.where(chosen[i][t], wanted[i], index)
                value = jnp.where(chosen[i][t], weight[i], value)
            meta_i = jnp.where(lane == t * K + k, index, meta_i)
            meta_w = jnp.where(lane == t * K + k, value, meta_w)
    mi_own[...] = meta_i
    mw_own[...] = meta_w
    mi_buf[0, core] = meta_i
    mw_buf[0, core] = meta_w

    for d in (1, 2, 3, 0):
        for c in (0, 1):
            if d == 0 and c == 1:
                continue
            for kind, (src, dst) in enumerate(((mi_own, mi_buf), (mw_own, mw_buf))):
                go(
                    remote(
                        src,
                        dst.at[(4 - d) % 4, core],
                        sem_m.at[0, kind, d, c],
                        sem_m.at[1, kind, (4 - d) % 4, core if d else 0],
                        device(x + d, y, z, c if d else other),
                    )
                )

    for ch in range(NCH):
        copy = pltpu.make_async_copy(
            teacher.at[0, :, rows(core, ch), :], raw[ch].at[pl.ds(core * 8, 8)], sem_own.at[ch]
        )
        copy.start()
        own[ch] = copy
        cross[ch] = go(
            remote(
                teacher.at[0, :, rows(other, ch), :],
                raw[ch].at[pl.ds(core * 8, 8)],
                sem_core.at[0, ch],
                sem_core.at[1, ch],
                partner,
            )
        )
    start_far(2)

    loads[0].wait()
    spot = lax.broadcasted_iota(jnp.int32, (64, 1024), 1)
    line = lax.broadcasted_iota(jnp.int32, (64, 1024), 0) * 16
    for n, (side, at) in enumerate(((16, 0), (32, 15))):
        hot = (spot == line + at).astype(F32).astype(BF16)
        edge[n] = jnp.dot(
            hot, pad[1:65, side : side + 16].reshape(1024, C), preferred_element_type=F32
        ).astype(BF16)
    halos = []
    for n, (src, dst, where) in enumerate(
        (
            (grid.at[63], pad.at[0, 16:48], (lon_up, lat)),
            (grid.at[0], pad.at[65, 16:48], (lon_dn, lat)),
            (edge.at[1], lat_buf.at[0], (lon, lat_up)),
            (edge.at[0], lat_buf.at[1], (lon, lat_dn)),
            (edge.at[1, 48:64], cor_buf.at[0], (lon_up, lat_up)),
            (edge.at[0, 48:64], cor_buf.at[1], (lon_up, lat_dn)),
            (edge.at[1, 0:16], cor_buf.at[2], (lon_dn, lat_up)),
            (edge.at[0, 0:16], cor_buf.at[3], (lon_dn, lat_dn)),
        )
    ):
        halos.append(go(remote(src, dst, sem_h.at[0, n], sem_h.at[1, n], where)))
    for ch in range(3, NCH):
        start_far(ch)

    for s in range(4):
        for c in (0, 1):
            if s == 0 and c == 1:
                continue
            for kind, (src, dst) in enumerate(((mi_own, mi_buf), (mw_own, mw_buf))):
                remote(
                    src, dst.at[s, c if s else other],
                    sem_m.at[0, kind, s, c], sem_m.at[1, kind, s, c], device(x + s, y, z, c),
                ).wait_recv()
    to_smem = [
        pltpu.make_async_copy(mi_buf, mi_smem, sem_ms.at[0]),
        pltpu.make_async_copy(mw_buf, mw_smem, sem_ms.at[1]),
    ]
    for copy in to_smem:
        copy.start()
    for copy in halos:
        copy.wait_recv()
    low = (lat > 0).astype(F32)
    high = (lat < 7).astype(F32)
    low_rows = (lat_buf[0].astype(F32) * low).reshape(64, 1, C)
    high_rows = (lat_buf[1].astype(F32) * high).reshape(64, 1, C)
    pad[1:65, 0:16] = jnp.broadcast_to(low_rows, (64, 16, C)).astype(BF16)
    pad[1:65, 48:64] = jnp.broadcast_to(high_rows, (64, 16, C)).astype(BF16)
    for n, (row, at, side, ok) in enumerate(
        ((15, 0, 0, low), (15, 0, 48, high), (0, 65, 0, low), (0, 65, 48, high))
    ):
        value = cor_buf[n].astype(F32)[row : row + 1] * ok
        pad[at, side : side + 16] = jnp.broadcast_to(value, (16, C)).astype(BF16)
    for copy in to_smem:
        copy.wait()
    loads[1].wait()
    loads[2].wait()

    def pick(d, c, t, k):
        g = mi_smem[d, c, 0, t * 2 + k]
        w = mw_smem[d, c, 0, t * 2 + k]
        owner, block = g // 8, g % 8
        o_core, o_x, o_yhi = owner % 2, (owner // 2) % 4, owner // 8
        where = o_core * 8 + block + jnp.where(o_yhi == y // 2, 0, 16)
        return where, jnp.where(o_x == x, w, 0.0)

    def weigh(ch):
        own[ch].wait()
        cross[ch].wait_recv()
        far_arrived(ch)
        for d in range(4):

            def one(n, carry, d=d):
                c, t = n // 4, n % 4
                i0, w0 = pick(d, c, t, 0)
                i1, w1 = pick(d, c, t, 1)
                total = w0 * raw[ch][i0].astype(F32) + w1 * raw[ch][i1].astype(F32)
                send[ch, d * 8 + n] = total.astype(BF16)
                return carry

            lax.fori_loop(0, 8, one, 0)

    def start_x(ch):
        for d in (2, 1, 3):
            for c in (0, 1):
                go(
                    remote(
                        send.at[ch, d * 8 + c * 4 : d * 8 + c * 4 + 4],
                        sums.at[4 - d, :, rows(core, ch), :],
                        sem_x1.at[0, ch, d - 1, c],
                        sem_x1.at[1, ch, d - 1, core],
                        device(x + d, y, z, c),
                    )
                )
        go(
            remote(
                send.at[ch, pl.ds(other * 4, 4)],
                sums.at[0, :, rows(core, ch), :],
                sem_x0.at[0, ch],
                sem_x0.at[1, ch],
                partner,
            )
        )
        copy = pltpu.make_async_copy(
            send.at[ch, pl.ds(core * 4, 4)], sums.at[0, :, rows(core, ch), :], sem_x0.at[2, ch]
        )
        copy.start()
        own[ch, "x"] = copy

    tiles = []
    for t in range(SLOTS):
        tile = jnp.int32(0)
        for i in range(8):
            tile = jnp.where(chosen[i][t], i, tile)
        tiles.append(tile)

    def shift(m, carry):
        tile, n = m // 18, m % 18
        a, b = tile // 2, tile % 2
        row = pad[a * 16 + n, pl.ds(pl.multiple_of(b * 16, 16), 48), :].astype(F32)
        at = pl.ds(pl.multiple_of(n * 16, 16), 16)
        xs[0, tile, at, :] = pltpu.roll(row, 1, 0)[16:32].astype(BF16)
        xs[1, tile, at, :] = row[16:32].astype(BF16)
        xs[2, tile, at, :] = pltpu.roll(row, 47, 0)[16:32].astype(BF16)
        return carry

    def forward(t):
        pre = jnp.zeros((256, C), F32)
        for tap in range(9):
            lon_step, lat_step = divmod(tap, 3)
            pre = pre + jnp.dot(
                xs[lat_step, tiles[t], lon_step * 16 : lon_step * 16 + 256, :],
                wbuf[tap],
                preferred_element_type=F32,
            )
        hidden = (pre * jax.nn.sigmoid(pre)).astype(BF16)
        pre_buf[t] = pre
        hid[t] = hidden
        full = xs[1, tiles[t], 16:272, :].astype(F32) + jnp.dot(
            hidden, mbuf[...], preferred_element_type=F32
        )
        full_buf[t] = full
        next_buf[t] = full.astype(BF16)

    lax.fori_loop(0, 144, shift, 0)
    for ch in range(NCH):
        weigh(ch)
        start_x(ch)
        if ch < SLOTS:
            forward(ch)

    for ch in range(NCH):
        for h in (0, 1):
            for d in (1, 2, 3):
                remote(
                    send.at[ch, 0:4],
                    sums.at[4 - d, :, rows(h, ch), :],
                    sem_x1.at[0, ch, d - 1, h],
                    sem_x1.at[1, ch, d - 1, h],
                    device(x + 1, y, z, h),
                ).wait_recv()
        remote(
            send.at[ch, 0:4],
            sums.at[0, :, rows(other, ch), :],
            sem_x0.at[0, ch],
            sem_x0.at[1, ch],
            partner,
        ).wait_recv()
        own[ch, "x"].wait()

    def backward(t, carry):
        pre = pre_buf[t]
        sig = jax.nn.sigmoid(pre)
        target = sums[0, t].astype(F32)
        for n in range(1, 4):
            target = target + sums[n, t].astype(F32)
        error = (full_buf[t] - target) * (t < count).astype(F32)
        mis_buf[t] = error.astype(BF16)
        scaled = (error * scale).astype(BF16)
        back = lax.dot_general(
            scaled, mbuf[...], (((1,), (1,)), ((), ())), preferred_element_type=F32
        )
        sc[t] = scaled
        dp[t] = (back * sig * (1.0 + pre * (1.0 - sig))).astype(BF16)
        return carry

    lax.fori_loop(0, SLOTS, backward, 0)
    outs = [
        pltpu.make_async_copy(next_buf, next_out, sem_o.at[0]),
        pltpu.make_async_copy(mis_buf, mis_out, sem_o.at[1]),
    ]
    for copy in outs:
        copy.start()

    contract = (((0,), (0,)), ((), ()))
    for tap in range(10):
        lon_step, lat_step = divmod(tap, 3)
        if tap < 9:
            left = jnp.concatenate(
                [xs[lat_step, tile, lon_step * 16 : lon_step * 16 + 256, :] for tile in tiles]
            )
            right = dp[...].reshape(1024, C)
        else:
            left, right = hid[...].reshape(1024, C), sc[...].reshape(1024, C)
        grad = lax.dot_general(left, right, contract, preferred_element_type=F32)
        grads[tap * C : (tap + 1) * C, :] = grad
        gb[tap * C : (tap + 1) * C, :] = grad.astype(BF16)
    grads[10 * C : 2 * HALF, :] = jnp.zeros((2 * HALF - 10 * C, C), F32)
    gb[10 * C : 2 * HALF, :] = jnp.zeros((2 * HALF - 10 * C, C), BF16)

    def col(q):
        return pl.ds(q * 128, 128)

    def at1(q, r, half=None):
        start = lax.rem(place[q] + r, 4) * 512
        if half is not None:
            start = start + half * HALF
        return pl.ds(pl.multiple_of(start, 512), 512)

    first = {}
    for r in (2, 1, 3, 0):
        for q in range(3):
            first[r, q] = go(
                remote(
                    gb.at[at1(q, r, other), col(q)], rc.at[at1(q, r), col(q)],
                    sem_c.at[0, r, q], sem_c.at[1, r, q], partner,
                )
            )
    one = {}
    for r in (2, 1, 3):
        for q in range(3):
            first[r, q].wait_recv()
            s1[r - 1, q] = (grads[at1(q, r, core), col(q)] + rc[at1(q, r), col(q)].astype(F32)).astype(BF16)
            one[r, q] = go(
                remote(
                    s1.at[r - 1, q], r1.at[r - 1, q], sem_1.at[0, r - 1, q], sem_1.at[1, r - 1, q],
                    peer(q, r),
                )
            )
    for q in range(3):
        first[0, q].wait_recv()
        a1[q] = grads[at1(q, 0, core), col(q)] + rc[at1(q, 0), col(q)].astype(F32)
    two = {}
    for q in range(3):
        for r in (1, 2, 3):
            one[r, q].wait_recv()
        a1[q] = a1[q] + (
            (r1[0, q].astype(F32) + r1[1, q].astype(F32)) + r1[2, q].astype(F32)
        )
        d1 = (q + 1) % 3
        for r in (2, 1, 3):
            v = lax.rem(place[d1] + r, 4)
            two[r, q] = go(
                remote(
                    a1.at[q, pl.ds(pl.multiple_of(v * 128, 128), 128)], r2.at[r - 1, q],
                    sem_2.at[0, r - 1, q], sem_2.at[1, r - 1, q], peer(d1, r),
                )
            )
    three = {}
    for q in range(3):
        d1, d2 = (q + 1) % 3, (q + 2) % 3
        for r in (1, 2, 3):
            two[r, q].wait_recv()
        mine = a1[q, pl.ds(pl.multiple_of(place[d1] * 128, 128), 128), :]
        a2[q] = mine + ((r2[0, q] + r2[1, q]) + r2[2, q])
        for r in (2, 1, 3):
            v = lax.rem(place[d2] + r, 4)
            three[r, q] = go(
                remote(
                    a2.at[q, pl.ds(pl.multiple_of(v * 32, 32), 32)], r3.at[r - 1, q],
                    sem_3.at[0, r - 1, q], sem_3.at[1, r - 1, q], peer(d2, r),
                )
            )
    base = core * HALF

    def span(q, level, shift=0):
        dims = (q, (q + 1) % 3, (q + 2) % 3)
        sizes = (512, 128, 32)
        start = base
        for n in range(level):
            v = place[dims[n]]
            if n == level - 1 and shift:
                v = lax.rem(v + shift, 4)
            start = start + v * sizes[n]
        size = sizes[level - 1]
        return obuf.at[pl.ds(pl.multiple_of(start, size), size), col(q)]

    def spread(q, level, sem):
        dim = (q + level - 1) % 3
        return {
            r: go(
                remote(
                    span(q, level), span(q, level), sem.at[0, r - 1, q], sem.at[1, r - 1, q], peer(dim, r)
                )
            )
            for r in (2, 1, 3)
        }

    g3, g2, g1, gc = {}, {}, {}, {}
    for q in range(3):
        d2 = (q + 2) % 3
        for r in (1, 2, 3):
            three[r, q].wait_recv()
        mine = a2[q, pl.ds(pl.multiple_of(place[d2] * 32, 32), 32), :]
        final = mine + ((r3[0, q] + r3[1, q]) + r3[2, q])
        start = base + place[q] * 512 + place[(q + 1) % 3] * 128 + place[d2] * 32
        obuf[pl.ds(pl.multiple_of(start, 32), 32), col(q)] = final.astype(BF16)
        g3[q] = spread(q, 3, sem_g3)
    for q in range(3):
        for r in (1, 2, 3):
            g3[q][r].wait_recv()
        g2[q] = spread(q, 2, sem_g2)

    def give(q, r):
        piece = span(q, 1, r)
        gc[q, r] = go(remote(piece, piece, sem_gc.at[0, r, q], sem_gc.at[1, r, q], partner))

    for q in range(3):
        for r in (1, 2, 3):
            g2[q][r].wait_recv()
        g1[q] = spread(q, 1, sem_g1)
        give(q, 0)
    for r in (1, 3, 2):
        for q in range(3):
            g1[q][r].wait_recv()
            give(q, 4 - r)
    for r in range(4):
        for q in range(3):
            gc[q, r].wait_recv()
    outs += [
        pltpu.make_async_copy(obuf.at[0 : 9 * C], conv_out, sem_o.at[2]),
        pltpu.make_async_copy(obuf.at[9 * C : 10 * C], mix_out, sem_o.at[3]),
    ]
    for copy in outs[2:]:
        copy.start()
    for copy in pend:
        copy.wait_send()
    for copy in outs:
        copy.wait()


def step(tile_mask, source_owner, source_block, margin_weight, grid, teacher, conv, mix, scale):
    anywhere = pl.BlockSpec(memory_space=pl.ANY)
    smem = pl.BlockSpec(memory_space=pltpu.SMEM)
    dma = pltpu.SemaphoreType.DMA
    return pl.pallas_call(
        functools.partial(step_kernel, scale=scale),
        out_shape=(
            jax.ShapeDtypeStruct((SLOTS, 256, C), BF16),
            jax.ShapeDtypeStruct((SLOTS, 256, C), BF16),
            jax.ShapeDtypeStruct((9 * C, C), BF16),
            jax.ShapeDtypeStruct((C, C), BF16),
        ),
        in_specs=[smem] * 4 + [anywhere] * 4,
        out_specs=(anywhere,) * 4,
        scratch_shapes=[
            pltpu.VMEM((8, 128), jnp.int32),
            pltpu.VMEM((8, 128), F32),
            pltpu.VMEM((4, 2, 8, 128), jnp.int32),
            pltpu.VMEM((4, 2, 8, 128), F32),
            pltpu.SMEM((4, 2, 8, 128), jnp.int32),
            pltpu.SMEM((4, 2, 8, 128), F32),
            pltpu.VMEM((NCH, 32, CR, C), BF16),
            pltpu.VMEM((4, SLOTS, 256, C), BF16),
            pltpu.VMEM((66, 64, C), BF16),
            pltpu.VMEM((2, 64, C), BF16),
            pltpu.VMEM((4, 16, C), BF16),
            pltpu.VMEM((2, 64, C), BF16),
            pltpu.VMEM((9, C, C), BF16),
            pltpu.VMEM((C, C), BF16),
            pltpu.VMEM((3, 8, 288, C), BF16),
            pltpu.VMEM((SLOTS, 256, C), F32),
            pltpu.VMEM((SLOTS, 256, C), F32),
            pltpu.VMEM((SLOTS, 256, C), BF16),
            pltpu.VMEM((SLOTS, 256, C), BF16),
            pltpu.VMEM((SLOTS, 256, C), BF16),
            pltpu.VMEM((SLOTS, 256, C), BF16),
            pltpu.VMEM((SLOTS, 256, C), BF16),
            pltpu.VMEM((2 * HALF, C), F32),
            pltpu.VMEM((2 * HALF, C), BF16),
            pltpu.VMEM((HALF, C), BF16),
            pltpu.VMEM((3, 3, 512, 128), BF16),
            pltpu.VMEM((3, 3, 512, 128), BF16),
            pltpu.VMEM((3, 512, 128), F32),
            pltpu.VMEM((3, 3, 128, 128), F32),
            pltpu.VMEM((3, 128, 128), F32),
            pltpu.VMEM((3, 3, 32, 128), F32),
            pltpu.VMEM((2 * HALF, C), BF16),
            dma((3,)),
            dma((2, 2, 4, 2)),
            dma((2,)),
            dma((2, 8)),
            dma((NCH,)),
            dma((2, NCH)),
            dma((2, NCH, 2)),
            dma((2, NCH, 3, 2)),
            dma((3, NCH)),
            dma((2, 4, 3)),
            dma((2, 3, 3)),
            dma((2, 3, 3)),
            dma((2, 3, 3)),
            dma((2, 3, 3)),
            dma((2, 3, 3)),
            dma((2, 3, 3)),
            dma((2, 4, 3)),
            dma((4,)),
        ]
        + [pltpu.VMEM((32, CR, C), BF16)] * NCH,
        compiler_params=pltpu.CompilerParams(
            collective_id=0, has_side_effects=True, vmem_limit_bytes=60 * 1024 * 1024
        ),
    )(tile_mask, source_owner, source_block, margin_weight, grid, teacher, conv, mix)


def place_kernel(mask, next_in, mis_in, conv_in, mix_in, next_ref, mis_ref, conv_ref, mix_ref):
    i = pl.program_id(0)
    slot = jnp.int32(0)
    for j in range(8):
        slot = slot + jnp.where(j < i, mask[j], 0)
    slot = jnp.minimum(slot, SLOTS - 1)
    ocean = mask[i] == 1

    @pl.when(ocean)
    def _():
        next_ref[...] = next_in[slot].reshape(TS, TS, C)
        mis_ref[...] = mis_in[slot].reshape(TS, TS, C)

    @pl.when(jnp.logical_not(ocean))
    def _():
        next_ref[...] = jnp.zeros_like(next_ref)
        mis_ref[...] = jnp.zeros_like(mis_ref)

    conv_ref[...] = conv_in[...].astype(F32)
    mix_ref[...] = mix_in[...].astype(F32)


def place_tiles(mask, next_in, mis_in, conv_in, mix_in):
    tile = pl.BlockSpec((TS, TS, C), lambda i, mask: (i // 2, i % 2, 0))
    whole = pl.BlockSpec((SLOTS, 256, C), lambda i, mask: (0, 0, 0))
    conv = pl.BlockSpec((9 * C // 8, C), lambda i, mask: (i, 0))
    mix = pl.BlockSpec((C // 8, C), lambda i, mask: (i, 0))
    return pl.pallas_call(
        place_kernel,
        out_shape=(
            jax.ShapeDtypeStruct((64, 32, C), BF16),
            jax.ShapeDtypeStruct((64, 32, C), BF16),
            jax.ShapeDtypeStruct((9 * C, C), F32),
            jax.ShapeDtypeStruct((C, C), F32),
        ),
        grid_spec=pltpu.PrefetchScalarGridSpec(
            num_scalar_prefetch=1,
            grid=(8,),
            in_specs=[whole, whole, conv, mix],
            out_specs=(tile, tile, conv, mix),
        ),
        compiler_params=pltpu.CompilerParams(dimension_semantics=("arbitrary",)),
    )(mask, next_in, mis_in, conv_in, mix_in)


def body(
    grid_state, conv_weight, mix_weight, teacher, tile_mask, source_owner, source_block, margin_weight
):
    width_lon, width_lat, chans = grid_state.shape
    cells = width_lon * lax.axis_size("lon") * width_lat * lax.axis_size("lat")
    parts = step(
        tile_mask, source_owner, source_block, margin_weight, grid_state, teacher,
        conv_weight, mix_weight, 1.0 / math.sqrt(cells),
    )
    next_state, misfit, grad_conv, grad_mix = place_tiles(tile_mask.reshape(8), *parts)
    return next_state, misfit, grad_conv.reshape(9, chans, chans), grad_mix


def solution(mesh):
    in_specs = (
        P("lon", "lat", None),
        P(),
        P(),
        P("lat", "lon", None, None),
        P("lon", "lat", None),
        P("lat", None, None),
        P("lat", None, None),
        P("lat", "lon", None),
    )
    out_specs = (P("lon", "lat", None), P("lon", "lat", None), P(), P())
    return jax.shard_map(body, mesh=mesh, in_specs=in_specs, out_specs=out_specs, check_vma=False)
```

```python
import functools
import math

import jax
import jax.numpy as jnp
from jax import lax
from jax.experimental import pallas as pl
from jax.experimental.pallas import tpu as pltpu
from jax.sharding import PartitionSpec as P

TS = 16
K = 2
SLOTS = 4
C = 384
NCH = 8
CR = 128 // NCH
HALF = 2048
SUBS = 2
PIECE = HALF // (4 * SUBS)
MESH = pl.DeviceIdType.MESH
F32 = jnp.float32
BF16 = jnp.bfloat16


def my_place():
    lon = lax.axis_index("lon")
    lat = lax.axis_index("lat")
    core = lax.rem(lon, 2)
    x = lax.rem(lax.div(lon, 2), 4)
    y = lax.div(lon, 8) * 2 + lax.div(lat, 4)
    z = lax.rem(lat, 4)
    return x, y, z, core


def device(x, y, z, core):
    x = lax.rem(x + 8, 4)
    y = lax.rem(y + 8, 4)
    z = lax.rem(z + 8, 4)
    return (lax.div(y, 2) * 8 + x * 2 + core, lax.rem(y, 2) * 4 + z)


def remote(src, dst, send, recv, where):
    return pltpu.make_async_remote_copy(
        src_ref=src, dst_ref=dst, send_sem=send, recv_sem=recv, device_id=where, device_id_type=MESH
    )


def greet(devices):
    barrier = pltpu.get_barrier_semaphore()
    for where in devices:
        pl.semaphore_signal(barrier, inc=1, device_id=where, device_id_type=MESH)
    pl.semaphore_wait(barrier, len(devices))


def step_kernel(
    mask_ref, owner_ref, block_ref, margin_ref, grid, teacher, conv, mix,
    next_out, mis_out, conv_out, mix_out,
    mi_own, mw_own, mi_buf, mw_buf, mi_smem, mw_smem, send, sums,
    pad, lat_buf, cor_buf, edge, wbuf, mbuf, xs, pre_buf, full_buf, hid, sc, dp, next_buf, mis_buf,
    grads, gb, rc, s1, r1, a1, r2, a2, r3, obuf,
    sem_in, sem_m, sem_ms, sem_h, sem_own, sem_core, sem_far, sem_x1, sem_x0,
    sem_c, sem_1, sem_2, sem_3, sem_g3, sem_g2, sem_g1, sem_gc, sem_o, *raw,
    scale,
):
    x, y, z, core = my_place()
    place = (x, y, z)
    other = 1 - core
    lon = lax.axis_index("lon")
    lat = lax.axis_index("lat")
    lon_up, lon_dn = lax.rem(lon + 1, 16), lax.rem(lon + 15, 16)
    lat_up, lat_dn = lax.rem(lat + 1, 8), lax.rem(lat + 7, 8)
    partner = device(x, y, z, other)

    def peer(dim, r):
        at = list(place)
        at[dim] = at[dim] + r
        return device(at[0], at[1], at[2], core)

    loads = [
        pltpu.make_async_copy(grid, pad.at[1:65, 16:48], sem_in.at[0]),
        pltpu.make_async_copy(conv, wbuf, sem_in.at[1]),
        pltpu.make_async_copy(mix, mbuf, sem_in.at[2]),
    ]
    for copy in loads:
        copy.start()

    greet(
        [partner, device(x, y + 2, z, other)]
        + [peer(d, r) for d in range(3) for r in (1, 2, 3)]
        + [device(x + s, y, z, other) for s in (1, 2, 3)]
        + [(lon_up, lat), (lon_dn, lat), (lon, lat_up), (lon, lat_dn)]
    )

    def rows(half, ch):
        return pl.ds(pl.multiple_of(half * 128 + ch * CR, CR), CR)

    far, own, cross, pend = {}, {}, {}, []

    def go(copy):
        copy.start()
        pend.append(copy)
        return copy

    def start_far(ch):
        for h in (0, 1):
            far[ch, h] = go(
                remote(
                    teacher.at[0, :, rows(h, ch), :],
                    raw[ch].at[pl.ds(16 + core * 8, 8)],
                    sem_far.at[0, ch, h],
                    sem_far.at[1, ch, core],
                    device(x, y + 2, z, h),
                )
            )

    def far_arrived(ch):
        for h in (0, 1):
            remote(
                teacher.at[0, :, rows(h, ch), :],
                raw[ch].at[16 + h * 8 : 24 + h * 8],
                sem_far.at[0, ch, h],
                sem_far.at[1, ch, h],
                device(x, y + 2, z, h),
            ).wait_recv()

    start_far(0)
    start_far(1)

    count = jnp.int32(0)
    chosen = []
    for i in range(8):
        on = mask_ref[0, 0, i]
        chosen.append([(on == 1) & (count == t) for t in range(SLOTS)])
        count = count + on
    lane = lax.broadcasted_iota(jnp.int32, (1, 128), 1)
    meta_i = jnp.zeros((1, 128), jnp.int32)
    meta_w = jnp.zeros((1, 128), F32)
    for k in range(K):
        wanted = [owner_ref[0, lon, i * K + k] * 8 + block_ref[0, lon, i * K + k] for i in range(8)]
        weight = [margin_ref[0, 0, i * K + k] for i in range(8)]
        for t in range(SLOTS):
            index, value = jnp.int32(0), jnp.float32(0)
            for i in range(8):
                index = jnp.where(chosen[i][t], wanted[i], index)
                value = jnp.where(chosen[i][t], weight[i], value)
            meta_i = jnp.where(lane == t * K + k, index, meta_i)
            meta_w = jnp.where(lane == t * K + k, value, meta_w)
    mi_own[...] = meta_i
    mw_own[...] = meta_w
    mi_buf[0, core] = meta_i
    mw_buf[0, core] = meta_w

    for d in (1, 2, 3, 0):
        for c in (0, 1):
            if d == 0 and c == 1:
                continue
            for kind, (src, dst) in enumerate(((mi_own, mi_buf), (mw_own, mw_buf))):
                go(
                    remote(
                        src,
                        dst.at[(4 - d) % 4, core],
                        sem_m.at[0, kind, d, c],
                        sem_m.at[1, kind, (4 - d) % 4, core if d else 0],
                        device(x + d, y, z, c if d else other),
                    )
                )

    for ch in range(NCH):
        copy = pltpu.make_async_copy(
            teacher.at[0, :, rows(core, ch), :], raw[ch].at[pl.ds(core * 8, 8)], sem_own.at[ch]
        )
        copy.start()
        own[ch] = copy
        cross[ch] = go(
            remote(
                teacher.at[0, :, rows(other, ch), :],
                raw[ch].at[pl.ds(core * 8, 8)],
                sem_core.at[0, ch],
                sem_core.at[1, ch],
                partner,
            )
        )
    start_far(2)

    loads[0].wait()
    spot = lax.broadcasted_iota(jnp.int32, (64, 1024), 1)
    line = lax.broadcasted_iota(jnp.int32, (64, 1024), 0) * 16
    for n, (side, at) in enumerate(((16, 0), (32, 15))):
        hot = (spot == line + at).astype(F32).astype(BF16)
        edge[n] = jnp.dot(
            hot, pad[1:65, side : side + 16].reshape(1024, C), preferred_element_type=F32
        ).astype(BF16)
    halos = []
    for n, (src, dst, where) in enumerate(
        (
            (grid.at[63], pad.at[0, 16:48], (lon_up, lat)),
            (grid.at[0], pad.at[65, 16:48], (lon_dn, lat)),
            (edge.at[1], lat_buf.at[0], (lon, lat_up)),
            (edge.at[0], lat_buf.at[1], (lon, lat_dn)),
        )
    ):
        halos.append(go(remote(src, dst, sem_h.at[0, n], sem_h.at[1, n], where)))
    for s in range(4):
        for c in (0, 1):
            if s == 0 and c == 1:
                continue
            for kind, (src, dst) in enumerate(((mi_own, mi_buf), (mw_own, mw_buf))):
                remote(
                    src, dst.at[s, c if s else other],
                    sem_m.at[0, kind, s, c], sem_m.at[1, kind, s, c], device(x + s, y, z, c),
                ).wait_recv()
    to_smem = [
        pltpu.make_async_copy(mi_buf, mi_smem, sem_ms.at[0]),
        pltpu.make_async_copy(mw_buf, mw_smem, sem_ms.at[1]),
    ]
    for copy in to_smem:
        copy.start()
    for copy in to_smem:
        copy.wait()

    def pick(d, c, t, k):
        g = mi_smem[d, c, 0, t * 2 + k]
        w = mw_smem[d, c, 0, t * 2 + k]
        owner, block = g // 8, g % 8
        o_core, o_x, o_yhi = owner % 2, (owner // 2) % 4, owner // 8
        where = o_core * 8 + block + jnp.where(o_yhi == y // 2, 0, 16)
        return where, jnp.where(o_x == x, w, 0.0)

    def weigh(ch):
        own[ch].wait()
        cross[ch].wait_recv()
        far_arrived(ch)
        for d in range(4):

            def one(n, carry, d=d):
                c, t = n // 4, n % 4
                i0, w0 = pick(d, c, t, 0)
                i1, w1 = pick(d, c, t, 1)
                total = w0 * raw[ch][i0].astype(F32) + w1 * raw[ch][i1].astype(F32)
                send[ch, d * 8 + n] = total.astype(BF16)
                return carry

            lax.fori_loop(0, 8, one, 0)

    def start_x(ch):
        for d in (2, 1, 3):
            for c in (0, 1):
                go(
                    remote(
                        send.at[ch, d * 8 + c * 4 : d * 8 + c * 4 + 4],
                        sums.at[4 - d, :, rows(core, ch), :],
                        sem_x1.at[0, ch, d - 1, c],
                        sem_x1.at[1, ch, d - 1, core],
                        device(x + d, y, z, c),
                    )
                )
        go(
            remote(
                send.at[ch, pl.ds(other * 4, 4)],
                sums.at[0, :, rows(core, ch), :],
                sem_x0.at[0, ch],
                sem_x0.at[1, ch],
                partner,
            )
        )
        copy = pltpu.make_async_copy(
            send.at[ch, pl.ds(core * 4, 4)], sums.at[0, :, rows(core, ch), :], sem_x0.at[2, ch]
        )
        copy.start()
        own[ch, "x"] = copy

    tiles = []
    for t in range(SLOTS):
        tile = jnp.int32(0)
        for i in range(8):
            tile = jnp.where(chosen[i][t], i, tile)
        tiles.append(tile)

    def shift(m, carry):
        tile, n = m // 18, m % 18
        a, b = tile // 2, tile % 2
        row = pad[a * 16 + n, pl.ds(pl.multiple_of(b * 16, 16), 48), :].astype(F32)
        at = pl.ds(pl.multiple_of(n * 16, 16), 16)
        xs[0, tile, at, :] = pltpu.roll(row, 1, 0)[16:32].astype(BF16)
        xs[1, tile, at, :] = row[16:32].astype(BF16)
        xs[2, tile, at, :] = pltpu.roll(row, 47, 0)[16:32].astype(BF16)
        return carry

    def forward(t):
        pre = jnp.zeros((256, C), F32)
        for tap in range(9):
            lon_step, lat_step = divmod(tap, 3)
            pre = pre + jnp.dot(
                xs[lat_step, tiles[t], lon_step * 16 : lon_step * 16 + 256, :],
                wbuf[tap],
                preferred_element_type=F32,
            )
        hidden = (pre * jax.nn.sigmoid(pre)).astype(BF16)
        pre_buf[t] = pre
        hid[t] = hidden
        full = xs[1, tiles[t], 16:272, :].astype(F32) + jnp.dot(
            hidden, mbuf[...], preferred_element_type=F32
        )
        full_buf[t] = full
        next_buf[t] = full.astype(BF16)

    def corners():
        for copy in halos[2:4]:
            copy.wait_recv()
        for n, (src, where) in enumerate(
            (
                (lat_buf.at[0, 48:64], (lon_up, lat)),
                (lat_buf.at[1, 48:64], (lon_up, lat)),
                (lat_buf.at[0, 0:16], (lon_dn, lat)),
                (lat_buf.at[1, 0:16], (lon_dn, lat)),
            )
        ):
            halos.append(
                go(remote(src, cor_buf.at[n], sem_h.at[0, 4 + n], sem_h.at[1, 4 + n], where))
            )

    def windows():
        for copy in halos[:2] + halos[4:]:
            copy.wait_recv()
        low = (lat > 0).astype(F32)
        high = (lat < 7).astype(F32)
        low_rows = (lat_buf[0].astype(F32) * low).reshape(64, 1, C)
        high_rows = (lat_buf[1].astype(F32) * high).reshape(64, 1, C)
        pad[1:65, 0:16] = jnp.broadcast_to(low_rows, (64, 16, C)).astype(BF16)
        pad[1:65, 48:64] = jnp.broadcast_to(high_rows, (64, 16, C)).astype(BF16)
        for n, (row, at, side, ok) in enumerate(
            ((15, 0, 0, low), (15, 0, 48, high), (0, 65, 0, low), (0, 65, 48, high))
        ):
            value = cor_buf[n].astype(F32)[row : row + 1] * ok
            pad[at, side : side + 16] = jnp.broadcast_to(value, (16, C)).astype(BF16)
        lax.fori_loop(0, 144, shift, 0)
        loads[1].wait()
        loads[2].wait()

    for ch in range(NCH):
        weigh(ch)
        if ch + 3 < NCH:
            start_far(ch + 3)
        start_x(ch)
        if ch == 0:
            corners()
        elif ch == 1:
            windows()
        elif ch < SLOTS + 2:
            forward(ch - 2)

    for ch in range(NCH):
        for h in (0, 1):
            for d in (1, 2, 3):
                remote(
                    send.at[ch, 0:4],
                    sums.at[4 - d, :, rows(h, ch), :],
                    sem_x1.at[0, ch, d - 1, h],
                    sem_x1.at[1, ch, d - 1, h],
                    device(x + 1, y, z, h),
                ).wait_recv()
        remote(
            send.at[ch, 0:4],
            sums.at[0, :, rows(other, ch), :],
            sem_x0.at[0, ch],
            sem_x0.at[1, ch],
            partner,
        ).wait_recv()
        own[ch, "x"].wait()

    def backward(t, carry):
        pre = pre_buf[t]
        sig = jax.nn.sigmoid(pre)
        target = sums[0, t].astype(F32)
        for n in range(1, 4):
            target = target + sums[n, t].astype(F32)
        error = (full_buf[t] - target) * (t < count).astype(F32)
        mis_buf[t] = error.astype(BF16)
        scaled = (error * scale).astype(BF16)
        back = lax.dot_general(
            scaled, mbuf[...], (((1,), (1,)), ((), ())), preferred_element_type=F32
        )
        sc[t] = scaled
        dp[t] = (back * sig * (1.0 + pre * (1.0 - sig))).astype(BF16)
        return carry

    lax.fori_loop(0, SLOTS, backward, 0)
    outs = [
        pltpu.make_async_copy(next_buf, next_out, sem_o.at[0]),
        pltpu.make_async_copy(mis_buf, mis_out, sem_o.at[1]),
    ]
    for copy in outs:
        copy.start()

    contract = (((0,), (0,)), ((), ()))
    for tap in range(10):
        lon_step, lat_step = divmod(tap, 3)
        if tap < 9:
            left = jnp.concatenate(
                [xs[lat_step, tile, lon_step * 16 : lon_step * 16 + 256, :] for tile in tiles]
            )
            right = dp[...].reshape(1024, C)
        else:
            left, right = hid[...].reshape(1024, C), sc[...].reshape(1024, C)
        grad = lax.dot_general(left, right, contract, preferred_element_type=F32)
        grads[tap * C : (tap + 1) * C, :] = grad
        gb[tap * C : (tap + 1) * C, :] = grad.astype(BF16)
    grads[10 * C : 2 * HALF, :] = jnp.zeros((2 * HALF - 10 * C, C), F32)
    gb[10 * C : 2 * HALF, :] = jnp.zeros((2 * HALF - 10 * C, C), BF16)

    def col(q):
        return pl.ds(q * 128, 128)

    def at1(p, r, half=None):
        start = (p // 3) * (HALF // SUBS) + lax.rem(place[p % 3] + r, 4) * PIECE
        if half is not None:
            start = start + half * HALF
        return pl.ds(pl.multiple_of(start, PIECE), PIECE)

    def dims(p):
        return p % 3, (p + 1) % 3, (p + 2) % 3

    groups = [range(3 * u, 3 * u + 3) for u in range(SUBS)]
    parts = range(3 * SUBS)
    sizes = (PIECE, PIECE // 4, PIECE // 16)
    first, one, two, three, g3, g2, g1, gc = {}, {}, {}, {}, {}, {}, {}, {}
    for group in groups:
        for r in (2, 1, 3, 0):
            for p in group:
                first[r, p] = go(
                    remote(
                        gb.at[at1(p, r, other), col(p % 3)], rc.at[at1(p, r), col(p % 3)],
                        sem_c.at[0, r, p], sem_c.at[1, r, p], partner,
                    )
                )
    for group in groups:
        for r in (2, 1, 3):
            for p in group:
                first[r, p].wait_recv()
                s1[r - 1, p] = (
                    grads[at1(p, r, core), col(p % 3)] + rc[at1(p, r), col(p % 3)].astype(F32)
                ).astype(BF16)
                one[r, p] = go(
                    remote(
                        s1.at[r - 1, p], r1.at[r - 1, p],
                        sem_1.at[0, r - 1, p], sem_1.at[1, r - 1, p], peer(p % 3, r),
                    )
                )
    for p in parts:
        first[0, p].wait_recv()
        a1[p] = grads[at1(p, 0, core), col(p % 3)] + rc[at1(p, 0), col(p % 3)].astype(F32)
    for p in parts:
        for r in (1, 2, 3):
            one[r, p].wait_recv()
        a1[p] = a1[p] + (
            (r1[0, p].astype(F32) + r1[1, p].astype(F32)) + r1[2, p].astype(F32)
        )
        d1 = dims(p)[1]
        for r in (2, 1, 3):
            v = lax.rem(place[d1] + r, 4)
            two[r, p] = go(
                remote(
                    a1.at[p, pl.ds(pl.multiple_of(v * sizes[1], sizes[1]), sizes[1])],
                    r2.at[r - 1, p],
                    sem_2.at[0, r - 1, p], sem_2.at[1, r - 1, p], peer(d1, r),
                )
            )
    for p in parts:
        _, d1, d2 = dims(p)
        for r in (1, 2, 3):
            two[r, p].wait_recv()
        mine = a1[p, pl.ds(pl.multiple_of(place[d1] * sizes[1], sizes[1]), sizes[1]), :]
        a2[p] = mine + ((r2[0, p] + r2[1, p]) + r2[2, p])
        for r in (2, 1, 3):
            v = lax.rem(place[d2] + r, 4)
            three[r, p] = go(
                remote(
                    a2.at[p, pl.ds(pl.multiple_of(v * sizes[2], sizes[2]), sizes[2])],
                    r3.at[r - 1, p],
                    sem_3.at[0, r - 1, p], sem_3.at[1, r - 1, p], peer(d2, r),
                )
            )

    def span(p, level, shift=0):
        start = core * HALF + (p // 3) * (HALF // SUBS)
        for n in range(level):
            v = place[dims(p)[n]]
            if n == level - 1 and shift:
                v = lax.rem(v + shift, 4)
            start = start + v * sizes[n]
        size = sizes[level - 1]
        return pl.ds(pl.multiple_of(start, size), size), col(p % 3)

    def spread(p, level, sem):
        dim = dims(p)[level - 1]
        piece = obuf.at[span(p, level)]
        return {
            r: go(remote(piece, piece, sem.at[0, r - 1, p], sem.at[1, r - 1, p], peer(dim, r)))
            for r in (2, 1, 3)
        }

    for p in parts:
        d2 = dims(p)[2]
        for r in (1, 2, 3):
            three[r, p].wait_recv()
        mine = a2[p, pl.ds(pl.multiple_of(place[d2] * sizes[2], sizes[2]), sizes[2]), :]
        final = mine + ((r3[0, p] + r3[1, p]) + r3[2, p])
        obuf[span(p, 3)] = final.astype(BF16)
        g3[p] = spread(p, 3, sem_g3)
    for p in parts:
        for r in (1, 2, 3):
            g3[p][r].wait_recv()
        g2[p] = spread(p, 2, sem_g2)

    def give(p, r):
        piece = obuf.at[span(p, 1, r)]
        gc[p, r] = go(remote(piece, piece, sem_gc.at[0, r, p], sem_gc.at[1, r, p], partner))

    for p in parts:
        for r in (1, 2, 3):
            g2[p][r].wait_recv()
        g1[p] = spread(p, 1, sem_g1)
        give(p, 0)
    for group in groups:
        for r in (1, 3, 2):
            for p in group:
                g1[p][r].wait_recv()
                give(p, 4 - r)
    for r in range(4):
        for p in parts:
            gc[p, r].wait_recv()
    outs += [
        pltpu.make_async_copy(obuf.at[0 : 9 * C], conv_out, sem_o.at[2]),
        pltpu.make_async_copy(obuf.at[9 * C : 10 * C], mix_out, sem_o.at[3]),
    ]
    for copy in outs[2:]:
        copy.start()
    for copy in pend:
        copy.wait_send()
    for copy in outs:
        copy.wait()


def step(tile_mask, source_owner, source_block, margin_weight, grid, teacher, conv, mix, scale):
    anywhere = pl.BlockSpec(memory_space=pl.ANY)
    smem = pl.BlockSpec(memory_space=pltpu.SMEM)
    dma = pltpu.SemaphoreType.DMA
    return pl.pallas_call(
        functools.partial(step_kernel, scale=scale),
        out_shape=(
            jax.ShapeDtypeStruct((SLOTS, 256, C), BF16),
            jax.ShapeDtypeStruct((SLOTS, 256, C), BF16),
            jax.ShapeDtypeStruct((9 * C, C), BF16),
            jax.ShapeDtypeStruct((C, C), BF16),
        ),
        in_specs=[smem] * 4 + [anywhere] * 4,
        out_specs=(anywhere,) * 4,
        scratch_shapes=[
            pltpu.VMEM((1, 128), jnp.int32),
            pltpu.VMEM((1, 128), F32),
            pltpu.VMEM((4, 2, 1, 128), jnp.int32),
            pltpu.VMEM((4, 2, 1, 128), F32),
            pltpu.SMEM((4, 2, 1, 128), jnp.int32),
            pltpu.SMEM((4, 2, 1, 128), F32),
            pltpu.VMEM((NCH, 32, CR, C), BF16),
            pltpu.VMEM((4, SLOTS, 256, C), BF16),
            pltpu.VMEM((66, 64, C), BF16),
            pltpu.VMEM((2, 64, C), BF16),
            pltpu.VMEM((4, 16, C), BF16),
            pltpu.VMEM((2, 64, C), BF16),
            pltpu.VMEM((9, C, C), BF16),
            pltpu.VMEM((C, C), BF16),
            pltpu.VMEM((3, 8, 288, C), BF16),
            pltpu.VMEM((SLOTS, 256, C), F32),
            pltpu.VMEM((SLOTS, 256, C), F32),
            pltpu.VMEM((SLOTS, 256, C), BF16),
            pltpu.VMEM((SLOTS, 256, C), BF16),
            pltpu.VMEM((SLOTS, 256, C), BF16),
            pltpu.VMEM((SLOTS, 256, C), BF16),
            pltpu.VMEM((SLOTS, 256, C), BF16),
            pltpu.VMEM((2 * HALF, C), F32),
            pltpu.VMEM((2 * HALF, C), BF16),
            pltpu.VMEM((HALF, C), BF16),
            pltpu.VMEM((3, 3 * SUBS, PIECE, 128), BF16),
            pltpu.VMEM((3, 3 * SUBS, PIECE, 128), BF16),
            pltpu.VMEM((3 * SUBS, PIECE, 128), F32),
            pltpu.VMEM((3, 3 * SUBS, PIECE // 4, 128), F32),
            pltpu.VMEM((3 * SUBS, PIECE // 4, 128), F32),
            pltpu.VMEM((3, 3 * SUBS, PIECE // 16, 128), F32),
            pltpu.VMEM((2 * HALF, C), BF16),
            dma((3,)),
            dma((2, 2, 4, 2)),
            dma((2,)),
            dma((2, 8)),
            dma((NCH,)),
            dma((2, NCH)),
            dma((2, NCH, 2)),
            dma((2, NCH, 3, 2)),
            dma((3, NCH)),
            dma((2, 4, 3 * SUBS)),
            dma((2, 3, 3 * SUBS)),
            dma((2, 3, 3 * SUBS)),
            dma((2, 3, 3 * SUBS)),
            dma((2, 3, 3 * SUBS)),
            dma((2, 3, 3 * SUBS)),
            dma((2, 3, 3 * SUBS)),
            dma((2, 4, 3 * SUBS)),
            dma((4,)),
        ]
        + [pltpu.VMEM((32, CR, C), BF16)] * NCH,
        compiler_params=pltpu.CompilerParams(
            collective_id=0, has_side_effects=True, vmem_limit_bytes=60 * 1024 * 1024
        ),
    )(tile_mask, source_owner, source_block, margin_weight, grid, teacher, conv, mix)


def place_kernel(
    mask, next_in, mis_in, conv_in, mix_in, next_out, mis_out, conv_out, mix_out,
    next_buf, mis_buf, conv_buf, mix_buf, conv_wide, mix_wide, zero, sem_in, sem_conv, sem_out, sem_wide,
):
    loads = [
        pltpu.make_async_copy(next_in, next_buf, sem_in.at[0]),
        pltpu.make_async_copy(mis_in, mis_buf, sem_in.at[1]),
        pltpu.make_async_copy(mix_in, mix_buf, sem_in.at[2]),
    ]
    steps = [pltpu.make_async_copy(conv_in.at[n], conv_buf.at[n], sem_conv.at[n]) for n in range(9)]
    for copy in [steps[0]] + loads + steps[1:]:
        copy.start()
    zero[...] = jnp.zeros_like(zero)
    outs = []

    def tiles(kind, buf, out):
        loads[kind].wait()
        slot = jnp.int32(0)
        for i in range(8):
            a, b = i // 2, i % 2
            spot = out.at[a * TS : (a + 1) * TS, b * TS : (b + 1) * TS]
            done = sem_out.at[kind, i]
            real = pltpu.make_async_copy(buf.at[jnp.minimum(slot, SLOTS - 1)], spot, done)
            blank = pltpu.make_async_copy(zero, spot, done)

            @pl.when(mask[0, 0, i] == 1)
            def _(real=real):
                real.start()

            @pl.when(mask[0, 0, i] != 1)
            def _(blank=blank):
                blank.start()

            slot = slot + mask[0, 0, i]
            outs.append(blank)

    def widen(n):
        steps[n].wait()
        conv_wide[n] = conv_buf[n].astype(F32)
        copy = pltpu.make_async_copy(conv_wide.at[n], conv_out.at[n], sem_wide.at[n])
        copy.start()
        outs.append(copy)

    widen(0)
    tiles(0, next_buf, next_out)
    widen(1)
    tiles(1, mis_buf, mis_out)
    for n in range(2, 9):
        widen(n)
    loads[2].wait()
    mix_wide[...] = mix_buf[...].astype(F32)
    copy = pltpu.make_async_copy(mix_wide, mix_out, sem_wide.at[9])
    copy.start()
    outs.append(copy)
    for copy in outs:
        copy.wait()


def place_tiles(mask, next_in, mis_in, conv_in, mix_in):
    anywhere = pl.BlockSpec(memory_space=pl.ANY)
    dma = pltpu.SemaphoreType.DMA
    tiles = (SLOTS, TS, TS, C)
    return pl.pallas_call(
        place_kernel,
        out_shape=(
            jax.ShapeDtypeStruct((64, 32, C), BF16),
            jax.ShapeDtypeStruct((64, 32, C), BF16),
            jax.ShapeDtypeStruct((9, C, C), F32),
            jax.ShapeDtypeStruct((C, C), F32),
        ),
        in_specs=[pl.BlockSpec(memory_space=pltpu.SMEM)] + [anywhere] * 4,
        out_specs=(anywhere,) * 4,
        scratch_shapes=[
            pltpu.VMEM(tiles, BF16),
            pltpu.VMEM(tiles, BF16),
            pltpu.VMEM((9, C, C), BF16),
            pltpu.VMEM((C, C), BF16),
            pltpu.VMEM((9, C, C), F32),
            pltpu.VMEM((C, C), F32),
            pltpu.VMEM((TS, TS, C), BF16),
            dma((3,)),
            dma((9,)),
            dma((2, 8)),
            dma((10,)),
        ],
    )(mask, next_in.reshape(tiles), mis_in.reshape(tiles), conv_in.reshape(9, C, C), mix_in)


def body(
    grid_state, conv_weight, mix_weight, teacher, tile_mask, source_owner, source_block, margin_weight
):
    width_lon, width_lat, _ = grid_state.shape
    cells = width_lon * lax.axis_size("lon") * width_lat * lax.axis_size("lat")
    parts = step(
        tile_mask, source_owner, source_block, margin_weight, grid_state, teacher,
        conv_weight, mix_weight, 1.0 / math.sqrt(cells),
    )
    next_state, misfit, grad_conv, grad_mix = place_tiles(tile_mask, *parts)
    return next_state, misfit, grad_conv, grad_mix


def solution(mesh):
    in_specs = (
        P("lon", "lat", None),
        P(),
        P(),
        P("lat", "lon", None, None),
        P("lon", "lat", None),
        P("lat", None, None),
        P("lat", None, None),
        P("lat", "lon", None),
    )
    out_specs = (P("lon", "lat", None), P("lon", "lat", None), P(), P())
    return jax.shard_map(body, mesh=mesh, in_specs=in_specs, out_specs=out_specs, check_vma=False)
```

```python
import functools
import math

import jax
import jax.numpy as jnp
from jax import lax
from jax.experimental import pallas as pl
from jax.experimental.pallas import tpu as pltpu
from jax.sharding import PartitionSpec as P

TS = 16
K = 2
SLOTS = 4
C = 384
NCH = 8
CR = 128 // NCH
HALF = 2048
SUBS = 2
PIECE = HALF // (4 * SUBS)
MESH = pl.DeviceIdType.MESH
F32 = jnp.float32
BF16 = jnp.bfloat16


def my_place():
    lon = lax.axis_index("lon")
    lat = lax.axis_index("lat")
    core = lax.rem(lon, 2)
    x = lax.rem(lax.div(lon, 2), 4)
    y = lax.div(lon, 8) * 2 + lax.div(lat, 4)
    z = lax.rem(lat, 4)
    return x, y, z, core


def device(x, y, z, core):
    x = lax.rem(x + 8, 4)
    y = lax.rem(y + 8, 4)
    z = lax.rem(z + 8, 4)
    return (lax.div(y, 2) * 8 + x * 2 + core, lax.rem(y, 2) * 4 + z)


def remote(src, dst, send, recv, where):
    return pltpu.make_async_remote_copy(
        src_ref=src, dst_ref=dst, send_sem=send, recv_sem=recv, device_id=where, device_id_type=MESH
    )


def greet(devices):
    barrier = pltpu.get_barrier_semaphore()
    for where in devices:
        pl.semaphore_signal(barrier, inc=1, device_id=where, device_id_type=MESH)
    pl.semaphore_wait(barrier, len(devices))


def step_kernel(
    mask_ref, owner_ref, block_ref, margin_ref, grid, teacher, conv, mix,
    next_out, mis_out, total_out,
    mi_own, mw_own, mi_buf, mw_buf, mi_smem, mw_smem, send, sums,
    pad, lat_buf, cor_buf, edge, wbuf, mbuf, xs, pre_buf, full_buf, hid, sc, dp, next_buf, mis_buf,
    grads, gb, rc, s1, r1, a1, r2, a2, r3, obuf,
    sem_in, sem_m, sem_ms, sem_h, sem_own, sem_core, sem_far, sem_x1, sem_x0,
    sem_c, sem_1, sem_2, sem_3, sem_g3, sem_g2, sem_g1, sem_gc, sem_o, sem_k, *raw,
    scale,
):
    x, y, z, core = my_place()
    place = (x, y, z)
    other = 1 - core
    lon = lax.axis_index("lon")
    lat = lax.axis_index("lat")
    lon_up, lon_dn = lax.rem(lon + 1, 16), lax.rem(lon + 15, 16)
    lat_up, lat_dn = lax.rem(lat + 1, 8), lax.rem(lat + 7, 8)
    partner = device(x, y, z, other)

    def peer(dim, r):
        at = list(place)
        at[dim] = at[dim] + r
        return device(at[0], at[1], at[2], core)

    loads = [
        pltpu.make_async_copy(grid, pad.at[1:65, 16:48], sem_in.at[0]),
        pltpu.make_async_copy(conv, wbuf, sem_in.at[1]),
        pltpu.make_async_copy(mix, mbuf, sem_in.at[2]),
    ]
    for copy in loads:
        copy.start()

    greet(
        [partner, device(x, y + 2, z, other)]
        + [peer(d, r) for d in range(3) for r in (1, 2, 3)]
        + [device(x + s, y, z, other) for s in (1, 2, 3)]
        + [(lon_up, lat), (lon_dn, lat), (lon, lat_up), (lon, lat_dn)]
    )

    def rows(half, ch):
        return pl.ds(pl.multiple_of(half * 128 + ch * CR, CR), CR)

    far, own, cross, pend = {}, {}, {}, []

    def go(copy):
        copy.start()
        pend.append(copy)
        return copy

    def start_far(ch):
        for h in (0, 1):
            far[ch, h] = go(
                remote(
                    teacher.at[0, :, rows(h, ch), :],
                    raw[ch].at[pl.ds(16 + core * 8, 8)],
                    sem_far.at[0, ch, h],
                    sem_far.at[1, ch, core],
                    device(x, y + 2, z, h),
                )
            )

    def far_arrived(ch):
        for h in (0, 1):
            remote(
                teacher.at[0, :, rows(h, ch), :],
                raw[ch].at[16 + h * 8 : 24 + h * 8],
                sem_far.at[0, ch, h],
                sem_far.at[1, ch, h],
                device(x, y + 2, z, h),
            ).wait_recv()

    start_far(0)

    count = jnp.int32(0)
    chosen = []
    for i in range(8):
        on = mask_ref[0, 0, i]
        chosen.append([(on == 1) & (count == t) for t in range(SLOTS)])
        count = count + on
    lane = lax.broadcasted_iota(jnp.int32, (1, 128), 1)
    meta_i = jnp.zeros((1, 128), jnp.int32)
    meta_w = jnp.zeros((1, 128), F32)
    for k in range(K):
        wanted = [owner_ref[0, lon, i * K + k] * 8 + block_ref[0, lon, i * K + k] for i in range(8)]
        weight = [margin_ref[0, 0, i * K + k] for i in range(8)]
        for t in range(SLOTS):
            index, value = jnp.int32(0), jnp.float32(0)
            for i in range(8):
                index = jnp.where(chosen[i][t], wanted[i], index)
                value = jnp.where(chosen[i][t], weight[i], value)
            meta_i = jnp.where(lane == t * K + k, index, meta_i)
            meta_w = jnp.where(lane == t * K + k, value, meta_w)
    mi_own[...] = meta_i
    mw_own[...] = meta_w
    mi_buf[0, core] = meta_i
    mw_buf[0, core] = meta_w

    for d in (1, 2, 3, 0):
        for c in (0, 1):
            if d == 0 and c == 1:
                continue
            for kind, (src, dst) in enumerate(((mi_own, mi_buf), (mw_own, mw_buf))):
                go(
                    remote(
                        src,
                        dst.at[(4 - d) % 4, core],
                        sem_m.at[0, kind, d, c],
                        sem_m.at[1, kind, (4 - d) % 4, core if d else 0],
                        device(x + d, y, z, c if d else other),
                    )
                )

    for ch in range(NCH):
        copy = pltpu.make_async_copy(
            teacher.at[0, :, rows(core, ch), :], raw[ch].at[pl.ds(core * 8, 8)], sem_own.at[ch]
        )
        copy.start()
        own[ch] = copy
        cross[ch] = go(
            remote(
                teacher.at[0, :, rows(other, ch), :],
                raw[ch].at[pl.ds(core * 8, 8)],
                sem_core.at[0, ch],
                sem_core.at[1, ch],
                partner,
            )
        )
    loads[0].wait()
    spot = lax.broadcasted_iota(jnp.int32, (64, 1024), 1)
    line = lax.broadcasted_iota(jnp.int32, (64, 1024), 0) * 16
    for n, (side, at) in enumerate(((16, 0), (32, 15))):
        hot = (spot == line + at).astype(F32).astype(BF16)
        edge[n] = jnp.dot(
            hot, pad[1:65, side : side + 16].reshape(1024, C), preferred_element_type=F32
        ).astype(BF16)
    halos = []
    for n, (src, dst, where) in enumerate(
        (
            (grid.at[63], pad.at[0, 16:48], (lon_up, lat)),
            (grid.at[0], pad.at[65, 16:48], (lon_dn, lat)),
            (edge.at[1], lat_buf.at[0], (lon, lat_up)),
            (edge.at[0], lat_buf.at[1], (lon, lat_dn)),
        )
    ):
        halos.append(go(remote(src, dst, sem_h.at[0, n], sem_h.at[1, n], where)))
    start_far(1)
    for s in range(4):
        for c in (0, 1):
            if s == 0 and c == 1:
                continue
            for kind, (src, dst) in enumerate(((mi_own, mi_buf), (mw_own, mw_buf))):
                remote(
                    src, dst.at[s, c if s else other],
                    sem_m.at[0, kind, s, c], sem_m.at[1, kind, s, c], device(x + s, y, z, c),
                ).wait_recv()
    to_smem = [
        pltpu.make_async_copy(mi_buf, mi_smem, sem_ms.at[0]),
        pltpu.make_async_copy(mw_buf, mw_smem, sem_ms.at[1]),
    ]
    for copy in to_smem:
        copy.start()
    for copy in to_smem:
        copy.wait()

    def pick(d, c, t, k):
        g = mi_smem[d, c, 0, t * 2 + k]
        w = mw_smem[d, c, 0, t * 2 + k]
        owner, block = g // 8, g % 8
        o_core, o_x, o_yhi = owner % 2, (owner // 2) % 4, owner // 8
        where = o_core * 8 + block + jnp.where(o_yhi == y // 2, 0, 16)
        return where, jnp.where(o_x == x, w, 0.0)

    def weigh(ch):
        own[ch].wait()
        cross[ch].wait_recv()
        far_arrived(ch)
        for d in range(4):

            def one(n, carry, d=d):
                c, t = n // 4, n % 4
                i0, w0 = pick(d, c, t, 0)
                i1, w1 = pick(d, c, t, 1)
                total = w0 * raw[ch][i0].astype(F32) + w1 * raw[ch][i1].astype(F32)
                send[ch, d * 8 + n] = total.astype(BF16)
                return carry

            lax.fori_loop(0, 8, one, 0)

    def start_x(ch):
        for d in (2, 1, 3):
            for c in (0, 1):
                go(
                    remote(
                        send.at[ch, d * 8 + c * 4 : d * 8 + c * 4 + 4],
                        sums.at[4 - d, :, rows(core, ch), :],
                        sem_x1.at[0, ch, d - 1, c],
                        sem_x1.at[1, ch, d - 1, core],
                        device(x + d, y, z, c),
                    )
                )
        go(
            remote(
                send.at[ch, pl.ds(other * 4, 4)],
                sums.at[0, :, rows(core, ch), :],
                sem_x0.at[0, ch],
                sem_x0.at[1, ch],
                partner,
            )
        )
        copy = pltpu.make_async_copy(
            send.at[ch, pl.ds(core * 4, 4)], sums.at[0, :, rows(core, ch), :], sem_x0.at[2, ch]
        )
        copy.start()
        own[ch, "x"] = copy

    tiles = []
    for t in range(SLOTS):
        tile = jnp.int32(0)
        for i in range(8):
            tile = jnp.where(chosen[i][t], i, tile)
        tiles.append(tile)

    def shift(m, carry):
        tile, n = m // 18, m % 18
        a, b = tile // 2, tile % 2
        row = pad[a * 16 + n, pl.ds(pl.multiple_of(b * 16, 16), 48), :].astype(F32)
        at = pl.ds(pl.multiple_of(n * 16, 16), 16)
        xs[0, tile, at, :] = pltpu.roll(row, 1, 0)[16:32].astype(BF16)
        xs[1, tile, at, :] = row[16:32].astype(BF16)
        xs[2, tile, at, :] = pltpu.roll(row, 47, 0)[16:32].astype(BF16)
        return carry

    def forward(t):
        pre = jnp.zeros((256, C), F32)
        for tap in range(9):
            lon_step, lat_step = divmod(tap, 3)
            pre = pre + jnp.dot(
                xs[lat_step, tiles[t], lon_step * 16 : lon_step * 16 + 256, :],
                wbuf[tap],
                preferred_element_type=F32,
            )
        hidden = (pre * jax.nn.sigmoid(pre)).astype(BF16)
        pre_buf[t] = pre
        hid[t] = hidden
        full = xs[1, tiles[t], 16:272, :].astype(F32) + jnp.dot(
            hidden, mbuf[...], preferred_element_type=F32
        )
        full_buf[t] = full
        next_buf[t] = full.astype(BF16)

    def corners():
        for copy in halos[2:4]:
            copy.wait_recv()
        for n, (src, where) in enumerate(
            (
                (lat_buf.at[0, 48:64], (lon_up, lat)),
                (lat_buf.at[1, 48:64], (lon_up, lat)),
                (lat_buf.at[0, 0:16], (lon_dn, lat)),
                (lat_buf.at[1, 0:16], (lon_dn, lat)),
            )
        ):
            halos.append(
                go(remote(src, cor_buf.at[n], sem_h.at[0, 4 + n], sem_h.at[1, 4 + n], where))
            )

    def windows():
        for copy in halos[:2] + halos[4:]:
            copy.wait_recv()
        low = (lat > 0).astype(F32)
        high = (lat < 7).astype(F32)
        low_rows = (lat_buf[0].astype(F32) * low).reshape(64, 1, C)
        high_rows = (lat_buf[1].astype(F32) * high).reshape(64, 1, C)
        pad[1:65, 0:16] = jnp.broadcast_to(low_rows, (64, 16, C)).astype(BF16)
        pad[1:65, 48:64] = jnp.broadcast_to(high_rows, (64, 16, C)).astype(BF16)
        for n, (row, at, side, ok) in enumerate(
            ((15, 0, 0, low), (15, 0, 48, high), (0, 65, 0, low), (0, 65, 48, high))
        ):
            value = cor_buf[n].astype(F32)[row : row + 1] * ok
            pad[at, side : side + 16] = jnp.broadcast_to(value, (16, C)).astype(BF16)
        lax.fori_loop(0, 144, shift, 0)
        loads[1].wait()
        loads[2].wait()

    for ch in range(NCH):
        weigh(ch)
        if ch + 2 < NCH:
            start_far(ch + 2)
        start_x(ch)
        if ch == 1:
            corners()
        elif ch == 3:
            windows()
        for t in {4: (0,), 5: (1,), 6: (2,), 7: (3,)}.get(ch, ()):
            forward(t)

    def sums_arrived(ch):
        for h in (0, 1):
            for d in (1, 2, 3):
                remote(
                    send.at[ch, 0:4],
                    sums.at[4 - d, :, rows(h, ch), :],
                    sem_x1.at[0, ch, d - 1, h],
                    sem_x1.at[1, ch, d - 1, h],
                    device(x + 1, y, z, h),
                ).wait_recv()
        remote(
            send.at[ch, 0:4],
            sums.at[0, :, rows(other, ch), :],
            sem_x0.at[0, ch],
            sem_x0.at[1, ch],
            partner,
        ).wait_recv()
        own[ch, "x"].wait()

    def backward(t, lo, n):
        for h in (0, 1):
            at = slice(h * 128 + lo, h * 128 + lo + n)
            pre = pre_buf[t, at]
            sig = jax.nn.sigmoid(pre)
            target = sums[0, t, at].astype(F32)
            for m in range(1, 4):
                target = target + sums[m, t, at].astype(F32)
            error = (full_buf[t, at] - target) * (t < count).astype(F32)
            mis_buf[t, at] = error.astype(BF16)
            scaled = (error * scale).astype(BF16)
            back = lax.dot_general(
                scaled, mbuf[...], (((1,), (1,)), ((), ())), preferred_element_type=F32
            )
            sc[t, at] = scaled
            dp[t, at] = (back * sig * (1.0 + pre * (1.0 - sig))).astype(BF16)

    contract = (((0,), (0,)), ((), ()))

    def gradients(lo, n, more):
        picks = [(t, h * 128 + lo) for t in range(SLOTS) for h in (0, 1)]

        def gather(ref):
            return jnp.concatenate([ref[t, at : at + n] for t, at in picks])

        right = gather(dp)
        for tap in range(10):
            lon_step, lat_step = divmod(tap, 3)
            if tap < 9:
                left = jnp.concatenate(
                    [
                        xs[lat_step, tiles[t], lon_step * 16 + at : lon_step * 16 + at + n, :]
                        for t, at in picks
                    ]
                )
            else:
                left, right = gather(hid), gather(sc)
            grad = lax.dot_general(left, right, contract, preferred_element_type=F32)
            span = slice(tap * C, (tap + 1) * C)
            if more:
                grads[span] = grad
            else:
                grad = grads[span] + grad
                grads[span] = grad
                gb[span] = grad.astype(BF16)

    outs = [pltpu.make_async_copy(next_buf, next_out, sem_o.at[0])]
    outs[0].start()
    grads[10 * C : 2 * HALF, :] = jnp.zeros((2 * HALF - 10 * C, C), F32)
    gb[10 * C : 2 * HALF, :] = jnp.zeros((2 * HALF - 10 * C, C), BF16)
    for start, end, more in ((0, NCH - 2, True), (NCH - 2, NCH, False)):
        for ch in range(start, end):
            sums_arrived(ch)

        def each(t, carry, lo=start * CR, n=(end - start) * CR):
            backward(t, lo, n)
            return carry

        lax.fori_loop(0, SLOTS, each, 0)
        gradients(start * CR, (end - start) * CR, more)
    outs.append(pltpu.make_async_copy(mis_buf, mis_out, sem_o.at[1]))
    outs[1].start()

    def col(q):
        return pl.ds(q * 128, 128)

    def at1(p, r, half=None):
        start = (p // 3) * (HALF // SUBS) + lax.rem(place[p % 3] + r, 4) * PIECE
        if half is not None:
            start = start + half * HALF
        return pl.ds(pl.multiple_of(start, PIECE), PIECE)

    def dims(p):
        return p % 3, (p + 1) % 3, (p + 2) % 3

    groups = [range(3 * u, 3 * u + 3) for u in range(SUBS)]
    parts = range(3 * SUBS)
    sizes = (PIECE, PIECE // 4, PIECE // 16)
    first, one, two, three, g3, g2, g1, gc = {}, {}, {}, {}, {}, {}, {}, {}
    for group in groups:
        for r in (2, 1, 3, 0):
            for p in group:
                first[r, p] = go(
                    remote(
                        gb.at[at1(p, r, other), col(p % 3)], rc.at[at1(p, r), col(p % 3)],
                        sem_c.at[0, r, p], sem_c.at[1, r, p], partner,
                    )
                )
    for group in groups:
        for r in (2, 1, 3):
            for p in group:
                first[r, p].wait_recv()
                s1[r - 1, p] = (
                    grads[at1(p, r, core), col(p % 3)] + rc[at1(p, r), col(p % 3)].astype(F32)
                ).astype(BF16)
                one[r, p] = go(
                    remote(
                        s1.at[r - 1, p], r1.at[r - 1, p],
                        sem_1.at[0, r - 1, p], sem_1.at[1, r - 1, p], peer(p % 3, r),
                    )
                )
    for p in parts:
        first[0, p].wait_recv()
        a1[p] = grads[at1(p, 0, core), col(p % 3)] + rc[at1(p, 0), col(p % 3)].astype(F32)
    for p in parts:
        for r in (1, 2, 3):
            one[r, p].wait_recv()
        a1[p] = a1[p] + (
            (r1[0, p].astype(F32) + r1[1, p].astype(F32)) + r1[2, p].astype(F32)
        )
        d1 = dims(p)[1]
        for r in (2, 1, 3):
            v = lax.rem(place[d1] + r, 4)
            two[r, p] = go(
                remote(
                    a1.at[p, pl.ds(pl.multiple_of(v * sizes[1], sizes[1]), sizes[1])],
                    r2.at[r - 1, p],
                    sem_2.at[0, r - 1, p], sem_2.at[1, r - 1, p], peer(d1, r),
                )
            )
    for p in parts:
        _, d1, d2 = dims(p)
        for r in (1, 2, 3):
            two[r, p].wait_recv()
        mine = a1[p, pl.ds(pl.multiple_of(place[d1] * sizes[1], sizes[1]), sizes[1]), :]
        a2[p] = mine + ((r2[0, p] + r2[1, p]) + r2[2, p])
        for r in (2, 1, 3):
            v = lax.rem(place[d2] + r, 4)
            three[r, p] = go(
                remote(
                    a2.at[p, pl.ds(pl.multiple_of(v * sizes[2], sizes[2]), sizes[2])],
                    r3.at[r - 1, p],
                    sem_3.at[0, r - 1, p], sem_3.at[1, r - 1, p], peer(d2, r),
                )
            )

    def span(p, level, shift=0):
        start = core * HALF + (p // 3) * (HALF // SUBS)
        for n in range(level):
            v = place[dims(p)[n]]
            if n == level - 1 and shift:
                v = lax.rem(v + shift, 4)
            start = start + v * sizes[n]
        size = sizes[level - 1]
        return pl.ds(pl.multiple_of(start, size), size), col(p % 3)

    def spread(p, level, sem):
        dim = dims(p)[level - 1]
        piece = obuf.at[span(p, level)]
        return {
            r: go(remote(piece, piece, sem.at[0, r - 1, p], sem.at[1, r - 1, p], peer(dim, r)))
            for r in (2, 1, 3)
        }

    for p in parts:
        d2 = dims(p)[2]
        for r in (1, 2, 3):
            three[r, p].wait_recv()
        mine = a2[p, pl.ds(pl.multiple_of(place[d2] * sizes[2], sizes[2]), sizes[2]), :]
        final = mine + ((r3[0, p] + r3[1, p]) + r3[2, p])
        obuf[span(p, 3)] = final.astype(BF16)
        g3[p] = spread(p, 3, sem_g3)
    for p in parts:
        for r in (1, 2, 3):
            g3[p][r].wait_recv()
        g2[p] = spread(p, 2, sem_g2)

    def keep(half, p, r):
        piece = half_span(half, p, r)
        copy = pltpu.make_async_copy(obuf.at[piece], total_out.at[piece], sem_k.at[half, r, p])
        copy.start()
        outs.append(copy)

    def half_span(half, p, r):
        start = core if half == 0 else other
        start = start * HALF + (p // 3) * (HALF // SUBS) + lax.rem(place[p % 3] + r, 4) * PIECE
        return pl.ds(pl.multiple_of(start, PIECE), PIECE), col(p % 3)

    def give(p, r):
        piece = obuf.at[span(p, 1, r)]
        keep(0, p, r)
        gc[p, r] = go(remote(piece, piece, sem_gc.at[0, r, p], sem_gc.at[1, r, p], partner))

    for p in parts:
        for r in (1, 2, 3):
            g2[p][r].wait_recv()
        g1[p] = spread(p, 1, sem_g1)
        give(p, 0)
    for group in groups:
        for r in (1, 3, 2):
            for p in group:
                g1[p][r].wait_recv()
                give(p, 4 - r)
    for group in groups:
        for r in (0, 3, 1, 2):
            for p in group:
                gc[p, r].wait_recv()
                keep(1, p, r)
    for copy in pend:
        copy.wait_send()
    for copy in outs:
        copy.wait()


def step(tile_mask, source_owner, source_block, margin_weight, grid, teacher, conv, mix, scale):
    anywhere = pl.BlockSpec(memory_space=pl.ANY)
    smem = pl.BlockSpec(memory_space=pltpu.SMEM)
    dma = pltpu.SemaphoreType.DMA
    return pl.pallas_call(
        functools.partial(step_kernel, scale=scale),
        out_shape=(
            jax.ShapeDtypeStruct((SLOTS, 256, C), BF16),
            jax.ShapeDtypeStruct((SLOTS, 256, C), BF16),
            jax.ShapeDtypeStruct((2 * HALF, C), BF16),
        ),
        in_specs=[smem] * 4 + [anywhere] * 4,
        out_specs=(anywhere,) * 3,
        scratch_shapes=[
            pltpu.VMEM((1, 128), jnp.int32),
            pltpu.VMEM((1, 128), F32),
            pltpu.VMEM((4, 2, 1, 128), jnp.int32),
            pltpu.VMEM((4, 2, 1, 128), F32),
            pltpu.SMEM((4, 2, 1, 128), jnp.int32),
            pltpu.SMEM((4, 2, 1, 128), F32),
            pltpu.VMEM((NCH, 32, CR, C), BF16),
            pltpu.VMEM((4, SLOTS, 256, C), BF16),
            pltpu.VMEM((66, 64, C), BF16),
            pltpu.VMEM((2, 64, C), BF16),
            pltpu.VMEM((4, 16, C), BF16),
            pltpu.VMEM((2, 64, C), BF16),
            pltpu.VMEM((9, C, C), BF16),
            pltpu.VMEM((C, C), BF16),
            pltpu.VMEM((3, 8, 288, C), BF16),
            pltpu.VMEM((SLOTS, 256, C), F32),
            pltpu.VMEM((SLOTS, 256, C), F32),
            pltpu.VMEM((SLOTS, 256, C), BF16),
            pltpu.VMEM((SLOTS, 256, C), BF16),
            pltpu.VMEM((SLOTS, 256, C), BF16),
            pltpu.VMEM((SLOTS, 256, C), BF16),
            pltpu.VMEM((SLOTS, 256, C), BF16),
            pltpu.VMEM((2 * HALF, C), F32),
            pltpu.VMEM((2 * HALF, C), BF16),
            pltpu.VMEM((HALF, C), BF16),
            pltpu.VMEM((3, 3 * SUBS, PIECE, 128), BF16),
            pltpu.VMEM((3, 3 * SUBS, PIECE, 128), BF16),
            pltpu.VMEM((3 * SUBS, PIECE, 128), F32),
            pltpu.VMEM((3, 3 * SUBS, PIECE // 4, 128), F32),
            pltpu.VMEM((3 * SUBS, PIECE // 4, 128), F32),
            pltpu.VMEM((3, 3 * SUBS, PIECE // 16, 128), F32),
            pltpu.VMEM((2 * HALF, C), BF16),
            dma((3,)),
            dma((2, 2, 4, 2)),
            dma((2,)),
            dma((2, 8)),
            dma((NCH,)),
            dma((2, NCH)),
            dma((2, NCH, 2)),
            dma((2, NCH, 3, 2)),
            dma((3, NCH)),
            dma((2, 4, 3 * SUBS)),
            dma((2, 3, 3 * SUBS)),
            dma((2, 3, 3 * SUBS)),
            dma((2, 3, 3 * SUBS)),
            dma((2, 3, 3 * SUBS)),
            dma((2, 3, 3 * SUBS)),
            dma((2, 3, 3 * SUBS)),
            dma((2, 4, 3 * SUBS)),
            dma((2,)),
            dma((2, 4, 3 * SUBS)),
        ]
        + [pltpu.VMEM((32, CR, C), BF16)] * NCH,
        compiler_params=pltpu.CompilerParams(
            collective_id=0, has_side_effects=True, vmem_limit_bytes=60 * 1024 * 1024
        ),
    )(tile_mask, source_owner, source_block, margin_weight, grid, teacher, conv, mix)


def place_kernel(
    mask, next_in, mis_in, total, next_out, mis_out, conv_out, mix_out,
    next_buf, mis_buf, conv_buf, mix_buf, conv_wide, mix_wide, zero, sem_in, sem_conv, sem_out, sem_wide,
):
    loads = [
        pltpu.make_async_copy(next_in, next_buf, sem_in.at[0]),
        pltpu.make_async_copy(mis_in, mis_buf, sem_in.at[1]),
        pltpu.make_async_copy(total.at[9 * C : 10 * C], mix_buf, sem_in.at[2]),
    ]
    steps = [
        pltpu.make_async_copy(total.at[n * C : (n + 1) * C], conv_buf.at[n], sem_conv.at[n])
        for n in range(9)
    ]
    for copy in [steps[0]] + loads + steps[1:]:
        copy.start()
    zero[...] = jnp.zeros_like(zero)
    outs = []

    def tiles(kind, buf, out):
        loads[kind].wait()
        slot = jnp.int32(0)
        for i in range(8):
            a, b = i // 2, i % 2
            spot = out.at[a * TS : (a + 1) * TS, b * TS : (b + 1) * TS]
            done = sem_out.at[kind, i]
            real = pltpu.make_async_copy(buf.at[jnp.minimum(slot, SLOTS - 1)], spot, done)
            blank = pltpu.make_async_copy(zero, spot, done)

            @pl.when(mask[0, 0, i] == 1)
            def _(real=real):
                real.start()

            @pl.when(mask[0, 0, i] != 1)
            def _(blank=blank):
                blank.start()

            slot = slot + mask[0, 0, i]
            outs.append(blank)

    def widen(n):
        steps[n].wait()
        conv_wide[n] = conv_buf[n].astype(F32)
        copy = pltpu.make_async_copy(conv_wide.at[n], conv_out.at[n], sem_wide.at[n])
        copy.start()
        outs.append(copy)

    widen(0)
    tiles(0, next_buf, next_out)
    widen(1)
    tiles(1, mis_buf, mis_out)
    for n in range(2, 9):
        widen(n)
    loads[2].wait()
    mix_wide[...] = mix_buf[...].astype(F32)
    copy = pltpu.make_async_copy(mix_wide, mix_out, sem_wide.at[9])
    copy.start()
    outs.append(copy)
    for copy in outs:
        copy.wait()


def place_tiles(mask, next_in, mis_in, total):
    anywhere = pl.BlockSpec(memory_space=pl.ANY)
    dma = pltpu.SemaphoreType.DMA
    tiles = (SLOTS, TS, TS, C)
    return pl.pallas_call(
        place_kernel,
        out_shape=(
            jax.ShapeDtypeStruct((64, 32, C), BF16),
            jax.ShapeDtypeStruct((64, 32, C), BF16),
            jax.ShapeDtypeStruct((9, C, C), F32),
            jax.ShapeDtypeStruct((C, C), F32),
        ),
        in_specs=[pl.BlockSpec(memory_space=pltpu.SMEM)] + [anywhere] * 3,
        out_specs=(anywhere,) * 4,
        scratch_shapes=[
            pltpu.VMEM(tiles, BF16),
            pltpu.VMEM(tiles, BF16),
            pltpu.VMEM((9, C, C), BF16),
            pltpu.VMEM((C, C), BF16),
            pltpu.VMEM((9, C, C), F32),
            pltpu.VMEM((C, C), F32),
            pltpu.VMEM((TS, TS, C), BF16),
            dma((3,)),
            dma((9,)),
            dma((2, 8)),
            dma((10,)),
        ],
    )(mask, next_in.reshape(tiles), mis_in.reshape(tiles), total)


def body(
    grid_state, conv_weight, mix_weight, teacher, tile_mask, source_owner, source_block, margin_weight
):
    width_lon, width_lat, _ = grid_state.shape
    cells = width_lon * lax.axis_size("lon") * width_lat * lax.axis_size("lat")
    parts = step(
        tile_mask, source_owner, source_block, margin_weight, grid_state, teacher,
        conv_weight, mix_weight, 1.0 / math.sqrt(cells),
    )
    next_state, misfit, grad_conv, grad_mix = place_tiles(tile_mask, *parts)
    return next_state, misfit, grad_conv, grad_mix


def solution(mesh):
    in_specs = (
        P("lon", "lat", None),
        P(),
        P(),
        P("lat", "lon", None, None),
        P("lon", "lat", None),
        P("lat", None, None),
        P("lat", None, None),
        P("lat", "lon", None),
    )
    out_specs = (P("lon", "lat", None), P("lon", "lat", None), P(), P())
    return jax.shard_map(body, mesh=mesh, in_specs=in_specs, out_specs=out_specs, check_vma=False)
```

```python
import functools
import math

import jax
import jax.numpy as jnp
from jax import lax
from jax.experimental import pallas as pl
from jax.experimental.pallas import tpu as pltpu
from jax.sharding import PartitionSpec as P

TS = 16
K = 2
SLOTS = 4
C = 384
NCH = 8
CR = 128 // NCH
HALF = 2048
SUBS = 2
PIECE = HALF // (4 * SUBS)
MESH = pl.DeviceIdType.MESH
F32 = jnp.float32
BF16 = jnp.bfloat16


def my_place():
    lon = lax.axis_index("lon")
    lat = lax.axis_index("lat")
    core = lax.rem(lon, 2)
    x = lax.rem(lax.div(lon, 2), 4)
    y = lax.div(lon, 8) * 2 + lax.div(lat, 4)
    z = lax.rem(lat, 4)
    return x, y, z, core


def device(x, y, z, core):
    x = lax.rem(x + 8, 4)
    y = lax.rem(y + 8, 4)
    z = lax.rem(z + 8, 4)
    return (lax.div(y, 2) * 8 + x * 2 + core, lax.rem(y, 2) * 4 + z)


def remote(src, dst, send, recv, where):
    return pltpu.make_async_remote_copy(
        src_ref=src, dst_ref=dst, send_sem=send, recv_sem=recv, device_id=where, device_id_type=MESH
    )


def greet(devices):
    barrier = pltpu.get_barrier_semaphore()
    for where in devices:
        pl.semaphore_signal(barrier, inc=1, device_id=where, device_id_type=MESH)
    pl.semaphore_wait(barrier, len(devices))


def step_kernel(
    mask_ref, owner_ref, block_ref, margin_ref, grid, teacher, conv, mix,
    next_out, mis_out, total_out,
    mi_own, mw_own, mi_buf, mw_buf, mi_smem, mw_smem, send, sums,
    pad, lat_buf, cor_buf, edge, wbuf, mbuf, xs, pre_buf, full_buf, hid, sc, dp, next_buf, mis_buf,
    grads, gb, rc, s1, r1, a1, r2, a2, r3, obuf,
    sem_in, sem_m, sem_ms, sem_h, sem_own, sem_core, sem_far, sem_x1, sem_x0,
    sem_c, sem_1, sem_2, sem_3, sem_g3, sem_g2, sem_g1, sem_gc, sem_o, sem_k, *raw,
    scale,
):
    x, y, z, core = my_place()
    place = (x, y, z)
    other = 1 - core
    lon = lax.axis_index("lon")
    lat = lax.axis_index("lat")
    lon_up, lon_dn = lax.rem(lon + 1, 16), lax.rem(lon + 15, 16)
    lat_up, lat_dn = lax.rem(lat + 1, 8), lax.rem(lat + 7, 8)
    partner = device(x, y, z, other)

    def peer(dim, r):
        at = list(place)
        at[dim] = at[dim] + r
        return device(at[0], at[1], at[2], core)

    loads = [
        pltpu.make_async_copy(grid, pad.at[1:65, 16:48], sem_in.at[0]),
        pltpu.make_async_copy(conv, wbuf, sem_in.at[1]),
        pltpu.make_async_copy(mix, mbuf, sem_in.at[2]),
    ]
    for copy in loads:
        copy.start()

    greet(
        [partner, device(x, y + 2, z, other)]
        + [peer(d, r) for d in range(3) for r in (1, 2, 3)]
        + [device(x + s, y, z, other) for s in (1, 2, 3)]
        + [(lon_up, lat), (lon_dn, lat), (lon, lat_up), (lon, lat_dn)]
    )

    def rows(half, ch):
        return pl.ds(pl.multiple_of(half * 128 + ch * CR, CR), CR)

    far, own, cross, pend = {}, {}, {}, []

    def go(copy):
        copy.start()
        pend.append(copy)
        return copy

    def start_far(ch):
        for h in (0, 1):
            far[ch, h] = go(
                remote(
                    teacher.at[0, :, rows(h, ch), :],
                    raw[ch].at[pl.ds(16 + core * 8, 8)],
                    sem_far.at[0, ch, h],
                    sem_far.at[1, ch, core],
                    device(x, y + 2, z, h),
                )
            )

    def far_arrived(ch):
        for h in (0, 1):
            remote(
                teacher.at[0, :, rows(h, ch), :],
                raw[ch].at[16 + h * 8 : 24 + h * 8],
                sem_far.at[0, ch, h],
                sem_far.at[1, ch, h],
                device(x, y + 2, z, h),
            ).wait_recv()

    start_far(0)

    count = jnp.int32(0)
    chosen = []
    for i in range(8):
        on = mask_ref[0, 0, i]
        chosen.append([(on == 1) & (count == t) for t in range(SLOTS)])
        count = count + on
    lane = lax.broadcasted_iota(jnp.int32, (1, 128), 1)
    meta_i = jnp.zeros((1, 128), jnp.int32)
    meta_w = jnp.zeros((1, 128), F32)
    for k in range(K):
        wanted = [owner_ref[0, lon, i * K + k] * 8 + block_ref[0, lon, i * K + k] for i in range(8)]
        weight = [margin_ref[0, 0, i * K + k] for i in range(8)]
        for t in range(SLOTS):
            index, value = jnp.int32(0), jnp.float32(0)
            for i in range(8):
                index = jnp.where(chosen[i][t], wanted[i], index)
                value = jnp.where(chosen[i][t], weight[i], value)
            meta_i = jnp.where(lane == t * K + k, index, meta_i)
            meta_w = jnp.where(lane == t * K + k, value, meta_w)
    mi_own[...] = meta_i
    mw_own[...] = meta_w
    mi_buf[0, core] = meta_i
    mw_buf[0, core] = meta_w

    for d in (1, 2, 3, 0):
        for c in (0, 1):
            if d == 0 and c == 1:
                continue
            for kind, (src, dst) in enumerate(((mi_own, mi_buf), (mw_own, mw_buf))):
                go(
                    remote(
                        src,
                        dst.at[(4 - d) % 4, core],
                        sem_m.at[0, kind, d, c],
                        sem_m.at[1, kind, (4 - d) % 4, core if d else 0],
                        device(x + d, y, z, c if d else other),
                    )
                )

    for ch in range(NCH):
        copy = pltpu.make_async_copy(
            teacher.at[0, :, rows(core, ch), :], raw[ch].at[pl.ds(core * 8, 8)], sem_own.at[ch]
        )
        copy.start()
        own[ch] = copy
        cross[ch] = go(
            remote(
                teacher.at[0, :, rows(other, ch), :],
                raw[ch].at[pl.ds(core * 8, 8)],
                sem_core.at[0, ch],
                sem_core.at[1, ch],
                partner,
            )
        )
    loads[0].wait()
    spot = lax.broadcasted_iota(jnp.int32, (64, 1024), 1)
    line = lax.broadcasted_iota(jnp.int32, (64, 1024), 0) * 16
    for n, (side, at) in enumerate(((16, 0), (32, 15))):
        hot = (spot == line + at).astype(F32).astype(BF16)
        edge[n] = jnp.dot(
            hot, pad[1:65, side : side + 16].reshape(1024, C), preferred_element_type=F32
        ).astype(BF16)
    halos = []
    for n, (src, dst, where) in enumerate(
        (
            (grid.at[63], pad.at[0, 16:48], (lon_up, lat)),
            (grid.at[0], pad.at[65, 16:48], (lon_dn, lat)),
            (edge.at[1], lat_buf.at[0], (lon, lat_up)),
            (edge.at[0], lat_buf.at[1], (lon, lat_dn)),
        )
    ):
        halos.append(go(remote(src, dst, sem_h.at[0, n], sem_h.at[1, n], where)))
    start_far(1)
    for s in range(4):
        for c in (0, 1):
            if s == 0 and c == 1:
                continue
            for kind, (src, dst) in enumerate(((mi_own, mi_buf), (mw_own, mw_buf))):
                remote(
                    src, dst.at[s, c if s else other],
                    sem_m.at[0, kind, s, c], sem_m.at[1, kind, s, c], device(x + s, y, z, c),
                ).wait_recv()
    to_smem = [
        pltpu.make_async_copy(mi_buf, mi_smem, sem_ms.at[0]),
        pltpu.make_async_copy(mw_buf, mw_smem, sem_ms.at[1]),
    ]
    for copy in to_smem:
        copy.start()
    for copy in to_smem:
        copy.wait()

    def pick(d, c, t, k):
        g = mi_smem[d, c, 0, t * 2 + k]
        w = mw_smem[d, c, 0, t * 2 + k]
        owner, block = g // 8, g % 8
        o_core, o_x, o_yhi = owner % 2, (owner // 2) % 4, owner // 8
        where = o_core * 8 + block + jnp.where(o_yhi == y // 2, 0, 16)
        return where, jnp.where(o_x == x, w, 0.0)

    def weigh(ch):
        own[ch].wait()
        cross[ch].wait_recv()
        far_arrived(ch)
        for d in range(4):

            def one(n, carry, d=d):
                c, t = n // 4, n % 4
                i0, w0 = pick(d, c, t, 0)
                i1, w1 = pick(d, c, t, 1)
                total = w0 * raw[ch][i0].astype(F32) + w1 * raw[ch][i1].astype(F32)
                send[ch, d * 8 + n] = total.astype(BF16)
                return carry

            lax.fori_loop(0, 8, one, 0)

    def start_x(ch):
        for d in (2, 1, 3):
            for c in (0, 1):
                go(
                    remote(
                        send.at[ch, d * 8 + c * 4 : d * 8 + c * 4 + 4],
                        sums.at[4 - d, :, rows(core, ch), :],
                        sem_x1.at[0, ch, d - 1, c],
                        sem_x1.at[1, ch, d - 1, core],
                        device(x + d, y, z, c),
                    )
                )
        go(
            remote(
                send.at[ch, pl.ds(other * 4, 4)],
                sums.at[0, :, rows(core, ch), :],
                sem_x0.at[0, ch],
                sem_x0.at[1, ch],
                partner,
            )
        )
        copy = pltpu.make_async_copy(
            send.at[ch, pl.ds(core * 4, 4)], sums.at[0, :, rows(core, ch), :], sem_x0.at[2, ch]
        )
        copy.start()
        own[ch, "x"] = copy

    tiles = []
    for t in range(SLOTS):
        tile = jnp.int32(0)
        for i in range(8):
            tile = jnp.where(chosen[i][t], i, tile)
        tiles.append(tile)

    def shift(m, carry):
        tile, n = m // 18, m % 18
        a, b = tile // 2, tile % 2
        row = pad[a * 16 + n, pl.ds(pl.multiple_of(b * 16, 16), 48), :].astype(F32)
        at = pl.ds(pl.multiple_of(n * 16, 16), 16)
        xs[0, tile, at, :] = pltpu.roll(row, 1, 0)[16:32].astype(BF16)
        xs[1, tile, at, :] = row[16:32].astype(BF16)
        xs[2, tile, at, :] = pltpu.roll(row, 47, 0)[16:32].astype(BF16)
        return carry

    def forward(t):
        pre = jnp.zeros((256, C), F32)
        for tap in range(9):
            lon_step, lat_step = divmod(tap, 3)
            pre = pre + jnp.dot(
                xs[lat_step, tiles[t], lon_step * 16 : lon_step * 16 + 256, :],
                wbuf[tap],
                preferred_element_type=F32,
            )
        hidden = (pre * jax.nn.sigmoid(pre)).astype(BF16)
        pre_buf[t] = pre
        hid[t] = hidden
        full = xs[1, tiles[t], 16:272, :].astype(F32) + jnp.dot(
            hidden, mbuf[...], preferred_element_type=F32
        )
        full_buf[t] = full
        next_buf[t] = full.astype(BF16)

    def corners():
        for copy in halos[2:4]:
            copy.wait_recv()
        for n, (src, where) in enumerate(
            (
                (lat_buf.at[0, 48:64], (lon_up, lat)),
                (lat_buf.at[1, 48:64], (lon_up, lat)),
                (lat_buf.at[0, 0:16], (lon_dn, lat)),
                (lat_buf.at[1, 0:16], (lon_dn, lat)),
            )
        ):
            halos.append(
                go(remote(src, cor_buf.at[n], sem_h.at[0, 4 + n], sem_h.at[1, 4 + n], where))
            )

    def windows():
        for copy in halos[:2] + halos[4:]:
            copy.wait_recv()
        low = (lat > 0).astype(F32)
        high = (lat < 7).astype(F32)
        low_rows = (lat_buf[0].astype(F32) * low).reshape(64, 1, C)
        high_rows = (lat_buf[1].astype(F32) * high).reshape(64, 1, C)
        pad[1:65, 0:16] = jnp.broadcast_to(low_rows, (64, 16, C)).astype(BF16)
        pad[1:65, 48:64] = jnp.broadcast_to(high_rows, (64, 16, C)).astype(BF16)
        for n, (row, at, side, ok) in enumerate(
            ((15, 0, 0, low), (15, 0, 48, high), (0, 65, 0, low), (0, 65, 48, high))
        ):
            value = cor_buf[n].astype(F32)[row : row + 1] * ok
            pad[at, side : side + 16] = jnp.broadcast_to(value, (16, C)).astype(BF16)
        lax.fori_loop(0, 144, shift, 0)
        loads[1].wait()
        loads[2].wait()

    for ch in range(NCH):
        weigh(ch)
        if ch + 2 < NCH:
            start_far(ch + 2)
        start_x(ch)
        if ch == 1:
            corners()
        elif ch == 3:
            windows()
        for t in {5: (0,), 6: (1,), 7: (2, 3)}.get(ch, ()):
            forward(t)

    def sums_arrived(ch):
        for h in (0, 1):
            for d in (1, 2, 3):
                remote(
                    send.at[ch, 0:4],
                    sums.at[4 - d, :, rows(h, ch), :],
                    sem_x1.at[0, ch, d - 1, h],
                    sem_x1.at[1, ch, d - 1, h],
                    device(x + 1, y, z, h),
                ).wait_recv()
        remote(
            send.at[ch, 0:4],
            sums.at[0, :, rows(other, ch), :],
            sem_x0.at[0, ch],
            sem_x0.at[1, ch],
            partner,
        ).wait_recv()
        own[ch, "x"].wait()

    def backward(t, lo, n):
        for h in (0, 1):
            at = slice(h * 128 + lo, h * 128 + lo + n)
            pre = pre_buf[t, at]
            sig = jax.nn.sigmoid(pre)
            target = sums[0, t, at].astype(F32)
            for m in range(1, 4):
                target = target + sums[m, t, at].astype(F32)
            error = (full_buf[t, at] - target) * (t < count).astype(F32)
            mis_buf[t, at] = error.astype(BF16)
            scaled = (error * scale).astype(BF16)
            back = lax.dot_general(
                scaled, mbuf[...], (((1,), (1,)), ((), ())), preferred_element_type=F32
            )
            sc[t, at] = scaled
            dp[t, at] = (back * sig * (1.0 + pre * (1.0 - sig))).astype(BF16)

    contract = (((0,), (0,)), ((), ()))

    def gradients(lo, n, more):
        picks = [(t, h * 128 + lo) for t in range(SLOTS) for h in (0, 1)]

        def gather(ref):
            return jnp.concatenate([ref[t, at : at + n] for t, at in picks])

        right = gather(dp)
        for tap in range(10):
            lon_step, lat_step = divmod(tap, 3)
            if tap < 9:
                left = jnp.concatenate(
                    [
                        xs[lat_step, tiles[t], lon_step * 16 + at : lon_step * 16 + at + n, :]
                        for t, at in picks
                    ]
                )
            else:
                left, right = gather(hid), gather(sc)
            grad = lax.dot_general(left, right, contract, preferred_element_type=F32)
            span = slice(tap * C, (tap + 1) * C)
            if more:
                grads[span] = grad
            else:
                grad = grads[span] + grad
                grads[span] = grad
                gb[span] = grad.astype(BF16)

    outs = [pltpu.make_async_copy(next_buf, next_out, sem_o.at[0])]
    outs[0].start()
    grads[10 * C : 2 * HALF, :] = jnp.zeros((2 * HALF - 10 * C, C), F32)
    gb[10 * C : 2 * HALF, :] = jnp.zeros((2 * HALF - 10 * C, C), BF16)
    for start, end, more in ((0, NCH - 2, True), (NCH - 2, NCH, False)):
        for ch in range(start, end):
            sums_arrived(ch)

        def each(t, carry, lo=start * CR, n=(end - start) * CR):
            backward(t, lo, n)
            return carry

        lax.fori_loop(0, SLOTS, each, 0)
        gradients(start * CR, (end - start) * CR, more)
    outs.append(pltpu.make_async_copy(mis_buf, mis_out, sem_o.at[1]))
    outs[1].start()

    def col(q):
        return pl.ds(q * 128, 128)

    def at1(p, r, half=None):
        start = (p // 3) * (HALF // SUBS) + lax.rem(place[p % 3] + r, 4) * PIECE
        if half is not None:
            start = start + half * HALF
        return pl.ds(pl.multiple_of(start, PIECE), PIECE)

    def dims(p):
        return p % 3, (p + 1) % 3, (p + 2) % 3

    groups = [range(3 * u, 3 * u + 3) for u in range(SUBS)]
    parts = range(3 * SUBS)
    sizes = (PIECE, PIECE // 4, PIECE // 16)
    first, one, two, three, g3, g2, g1, gc = {}, {}, {}, {}, {}, {}, {}, {}
    for group in groups:
        for r in (2, 1, 3, 0):
            for p in group:
                first[r, p] = go(
                    remote(
                        gb.at[at1(p, r, other), col(p % 3)], rc.at[at1(p, r), col(p % 3)],
                        sem_c.at[0, r, p], sem_c.at[1, r, p], partner,
                    )
                )
    for group in groups:
        for r in (2, 1, 3):
            for p in group:
                first[r, p].wait_recv()
                s1[r - 1, p] = (
                    grads[at1(p, r, core), col(p % 3)] + rc[at1(p, r), col(p % 3)].astype(F32)
                ).astype(BF16)
                one[r, p] = go(
                    remote(
                        s1.at[r - 1, p], r1.at[r - 1, p],
                        sem_1.at[0, r - 1, p], sem_1.at[1, r - 1, p], peer(p % 3, r),
                    )
                )
    for p in parts:
        first[0, p].wait_recv()
        a1[p] = grads[at1(p, 0, core), col(p % 3)] + rc[at1(p, 0), col(p % 3)].astype(F32)
    for p in parts:
        for r in (1, 2, 3):
            one[r, p].wait_recv()
        a1[p] = a1[p] + (
            (r1[0, p].astype(F32) + r1[1, p].astype(F32)) + r1[2, p].astype(F32)
        )
        d1 = dims(p)[1]
        for r in (2, 1, 3):
            v = lax.rem(place[d1] + r, 4)
            two[r, p] = go(
                remote(
                    a1.at[p, pl.ds(pl.multiple_of(v * sizes[1], sizes[1]), sizes[1])],
                    r2.at[r - 1, p],
                    sem_2.at[0, r - 1, p], sem_2.at[1, r - 1, p], peer(d1, r),
                )
            )
    for p in parts:
        _, d1, d2 = dims(p)
        for r in (1, 2, 3):
            two[r, p].wait_recv()
        mine = a1[p, pl.ds(pl.multiple_of(place[d1] * sizes[1], sizes[1]), sizes[1]), :]
        a2[p] = mine + ((r2[0, p] + r2[1, p]) + r2[2, p])
        for r in (2, 1, 3):
            v = lax.rem(place[d2] + r, 4)
            three[r, p] = go(
                remote(
                    a2.at[p, pl.ds(pl.multiple_of(v * sizes[2], sizes[2]), sizes[2])],
                    r3.at[r - 1, p],
                    sem_3.at[0, r - 1, p], sem_3.at[1, r - 1, p], peer(d2, r),
                )
            )

    def span(p, level, shift=0):
        start = core * HALF + (p // 3) * (HALF // SUBS)
        for n in range(level):
            v = place[dims(p)[n]]
            if n == level - 1 and shift:
                v = lax.rem(v + shift, 4)
            start = start + v * sizes[n]
        size = sizes[level - 1]
        return pl.ds(pl.multiple_of(start, size), size), col(p % 3)

    def spread(p, level, sem):
        dim = dims(p)[level - 1]
        piece = obuf.at[span(p, level)]
        return {
            r: go(remote(piece, piece, sem.at[0, r - 1, p], sem.at[1, r - 1, p], peer(dim, r)))
            for r in (2, 1, 3)
        }

    for p in parts:
        d2 = dims(p)[2]
        for r in (1, 2, 3):
            three[r, p].wait_recv()
        mine = a2[p, pl.ds(pl.multiple_of(place[d2] * sizes[2], sizes[2]), sizes[2]), :]
        final = mine + ((r3[0, p] + r3[1, p]) + r3[2, p])
        obuf[span(p, 3)] = final.astype(BF16)
        g3[p] = spread(p, 3, sem_g3)
    for p in parts:
        for r in (1, 2, 3):
            g3[p][r].wait_recv()
        g2[p] = spread(p, 2, sem_g2)

    def keep(half, p, r):
        piece = half_span(half, p, r)
        copy = pltpu.make_async_copy(obuf.at[piece], total_out.at[piece], sem_k.at[half, r, p])
        copy.start()
        outs.append(copy)

    def half_span(half, p, r):
        start = core if half == 0 else other
        start = start * HALF + (p // 3) * (HALF // SUBS) + lax.rem(place[p % 3] + r, 4) * PIECE
        return pl.ds(pl.multiple_of(start, PIECE), PIECE), col(p % 3)

    def give(p, r):
        piece = obuf.at[span(p, 1, r)]
        keep(0, p, r)
        gc[p, r] = go(remote(piece, piece, sem_gc.at[0, r, p], sem_gc.at[1, r, p], partner))

    for p in parts:
        for r in (1, 2, 3):
            g2[p][r].wait_recv()
        g1[p] = spread(p, 1, sem_g1)
        give(p, 0)
    for group in groups:
        for r in (1, 3, 2):
            for p in group:
                g1[p][r].wait_recv()
                give(p, 4 - r)
    for group in groups:
        for r in (0, 3, 1, 2):
            for p in group:
                gc[p, r].wait_recv()
                keep(1, p, r)
    for copy in pend:
        copy.wait_send()
    for copy in outs:
        copy.wait()


def step(tile_mask, source_owner, source_block, margin_weight, grid, teacher, conv, mix, scale):
    anywhere = pl.BlockSpec(memory_space=pl.ANY)
    smem = pl.BlockSpec(memory_space=pltpu.SMEM)
    dma = pltpu.SemaphoreType.DMA
    return pl.pallas_call(
        functools.partial(step_kernel, scale=scale),
        out_shape=(
            jax.ShapeDtypeStruct((SLOTS, 256, C), BF16),
            jax.ShapeDtypeStruct((SLOTS, 256, C), BF16),
            jax.ShapeDtypeStruct((2 * HALF, C), BF16),
        ),
        in_specs=[smem] * 4 + [anywhere] * 4,
        out_specs=(anywhere,) * 3,
        scratch_shapes=[
            pltpu.VMEM((1, 128), jnp.int32),
            pltpu.VMEM((1, 128), F32),
            pltpu.VMEM((4, 2, 1, 128), jnp.int32),
            pltpu.VMEM((4, 2, 1, 128), F32),
            pltpu.SMEM((4, 2, 1, 128), jnp.int32),
            pltpu.SMEM((4, 2, 1, 128), F32),
            pltpu.VMEM((NCH, 32, CR, C), BF16),
            pltpu.VMEM((4, SLOTS, 256, C), BF16),
            pltpu.VMEM((66, 64, C), BF16),
            pltpu.VMEM((2, 64, C), BF16),
            pltpu.VMEM((4, 16, C), BF16),
            pltpu.VMEM((2, 64, C), BF16),
            pltpu.VMEM((9, C, C), BF16),
            pltpu.VMEM((C, C), BF16),
            pltpu.VMEM((3, 8, 288, C), BF16),
            pltpu.VMEM((SLOTS, 256, C), F32),
            pltpu.VMEM((SLOTS, 256, C), F32),
            pltpu.VMEM((SLOTS, 256, C), BF16),
            pltpu.VMEM((SLOTS, 256, C), BF16),
            pltpu.VMEM((SLOTS, 256, C), BF16),
            pltpu.VMEM((SLOTS, 256, C), BF16),
            pltpu.VMEM((SLOTS, 256, C), BF16),
            pltpu.VMEM((2 * HALF, C), F32),
            pltpu.VMEM((2 * HALF, C), BF16),
            pltpu.VMEM((HALF, C), BF16),
            pltpu.VMEM((3, 3 * SUBS, PIECE, 128), BF16),
            pltpu.VMEM((3, 3 * SUBS, PIECE, 128), BF16),
            pltpu.VMEM((3 * SUBS, PIECE, 128), F32),
            pltpu.VMEM((3, 3 * SUBS, PIECE // 4, 128), F32),
            pltpu.VMEM((3 * SUBS, PIECE // 4, 128), F32),
            pltpu.VMEM((3, 3 * SUBS, PIECE // 16, 128), F32),
            pltpu.VMEM((2 * HALF, C), BF16),
            dma((3,)),
            dma((2, 2, 4, 2)),
            dma((2,)),
            dma((2, 8)),
            dma((NCH,)),
            dma((2, NCH)),
            dma((2, NCH, 2)),
            dma((2, NCH, 3, 2)),
            dma((3, NCH)),
            dma((2, 4, 3 * SUBS)),
            dma((2, 3, 3 * SUBS)),
            dma((2, 3, 3 * SUBS)),
            dma((2, 3, 3 * SUBS)),
            dma((2, 3, 3 * SUBS)),
            dma((2, 3, 3 * SUBS)),
            dma((2, 3, 3 * SUBS)),
            dma((2, 4, 3 * SUBS)),
            dma((2,)),
            dma((2, 4, 3 * SUBS)),
        ]
        + [pltpu.VMEM((32, CR, C), BF16)] * NCH,
        compiler_params=pltpu.CompilerParams(
            collective_id=0, has_side_effects=True, vmem_limit_bytes=60 * 1024 * 1024
        ),
    )(tile_mask, source_owner, source_block, margin_weight, grid, teacher, conv, mix)


def place_kernel(
    mask, next_in, mis_in, total, next_out, mis_out, conv_out, mix_out,
    next_buf, mis_buf, conv_buf, mix_buf, conv_wide, mix_wide, zero, sem_in, sem_conv, sem_out, sem_wide,
):
    loads = [
        pltpu.make_async_copy(next_in, next_buf, sem_in.at[0]),
        pltpu.make_async_copy(mis_in, mis_buf, sem_in.at[1]),
        pltpu.make_async_copy(total.at[9 * C : 10 * C], mix_buf, sem_in.at[2]),
    ]
    steps = [
        pltpu.make_async_copy(total.at[n * C : (n + 1) * C], conv_buf.at[n], sem_conv.at[n])
        for n in range(9)
    ]
    for copy in [steps[0]] + loads + steps[1:]:
        copy.start()
    zero[...] = jnp.zeros_like(zero)
    outs = []

    def tiles(kind, buf, out):
        loads[kind].wait()
        slot = jnp.int32(0)
        for i in range(8):
            a, b = i // 2, i % 2
            spot = out.at[a * TS : (a + 1) * TS, b * TS : (b + 1) * TS]
            done = sem_out.at[kind, i]
            real = pltpu.make_async_copy(buf.at[jnp.minimum(slot, SLOTS - 1)], spot, done)
            blank = pltpu.make_async_copy(zero, spot, done)

            @pl.when(mask[0, 0, i] == 1)
            def _(real=real):
                real.start()

            @pl.when(mask[0, 0, i] != 1)
            def _(blank=blank):
                blank.start()

            slot = slot + mask[0, 0, i]
            outs.append(blank)

    def widen(n):
        steps[n].wait()
        conv_wide[n] = conv_buf[n].astype(F32)
        copy = pltpu.make_async_copy(conv_wide.at[n], conv_out.at[n], sem_wide.at[n])
        copy.start()
        outs.append(copy)

    widen(0)
    tiles(0, next_buf, next_out)
    widen(1)
    tiles(1, mis_buf, mis_out)
    for n in range(2, 9):
        widen(n)
    loads[2].wait()
    mix_wide[...] = mix_buf[...].astype(F32)
    copy = pltpu.make_async_copy(mix_wide, mix_out, sem_wide.at[9])
    copy.start()
    outs.append(copy)
    for copy in outs:
        copy.wait()


def place_tiles(mask, next_in, mis_in, total):
    anywhere = pl.BlockSpec(memory_space=pl.ANY)
    dma = pltpu.SemaphoreType.DMA
    tiles = (SLOTS, TS, TS, C)
    return pl.pallas_call(
        place_kernel,
        out_shape=(
            jax.ShapeDtypeStruct((64, 32, C), BF16),
            jax.ShapeDtypeStruct((64, 32, C), BF16),
            jax.ShapeDtypeStruct((9, C, C), F32),
            jax.ShapeDtypeStruct((C, C), F32),
        ),
        in_specs=[pl.BlockSpec(memory_space=pltpu.SMEM)] + [anywhere] * 3,
        out_specs=(anywhere,) * 4,
        scratch_shapes=[
            pltpu.VMEM(tiles, BF16),
            pltpu.VMEM(tiles, BF16),
            pltpu.VMEM((9, C, C), BF16),
            pltpu.VMEM((C, C), BF16),
            pltpu.VMEM((9, C, C), F32),
            pltpu.VMEM((C, C), F32),
            pltpu.VMEM((TS, TS, C), BF16),
            dma((3,)),
            dma((9,)),
            dma((2, 8)),
            dma((10,)),
        ],
    )(mask, next_in.reshape(tiles), mis_in.reshape(tiles), total)


def body(
    grid_state, conv_weight, mix_weight, teacher, tile_mask, source_owner, source_block, margin_weight
):
    width_lon, width_lat, _ = grid_state.shape
    cells = width_lon * lax.axis_size("lon") * width_lat * lax.axis_size("lat")
    parts = step(
        tile_mask, source_owner, source_block, margin_weight, grid_state, teacher,
        conv_weight, mix_weight, 1.0 / math.sqrt(cells),
    )
    next_state, misfit, grad_conv, grad_mix = place_tiles(tile_mask, *parts)
    return next_state, misfit, grad_conv, grad_mix


def solution(mesh):
    in_specs = (
        P("lon", "lat", None),
        P(),
        P(),
        P("lat", "lon", None, None),
        P("lon", "lat", None),
        P("lat", None, None),
        P("lat", None, None),
        P("lat", "lon", None),
    )
    out_specs = (P("lon", "lat", None), P("lon", "lat", None), P(), P())
    return jax.shard_map(body, mesh=mesh, in_specs=in_specs, out_specs=out_specs, check_vma=False)
```
